256 devices in a mesh: stream: 16 (over x, y), span: 8 (over z), grid: 2 (over core).
Axes of the slice: x: 4, y: 4, z: 8, core: 2. Of those that a mesh axis runs over, the one named last changes fastest.
Arguments:
- velocity: float32 [3, 2, 128, 256, 256], P(None, 'grid', 'stream', 'span'), may hold values from -2.5 to 2.5
- history: float32 [2, 2, 128, 256, 256], P(None, 'grid', 'stream', 'span'), may hold values from 0.1 to 10
- donor_rows: int32 [2, 16, 8, 128, 2, 2], P('grid', 'stream', 'span'), may hold values from 0 to 511
- recv_dest: int32 [2, 16, 8, 128, 2], P('grid', 'stream', 'span'), may hold values from 0 to 512, as said below
- recv_weight: float32 [2, 16, 8, 128, 2], P('grid', 'stream', 'span'), may hold values from 0 to 1
Outputs:
- history_new: float32 [2, 2, 128, 256, 256], P(None, 'grid', 'stream', 'span')
- eddy: float32 [2, 128, 256, 256], P('grid', 'stream', 'span')
The draws below stay inside these ranges and needn't reach their ends.
Inputs may be any that keep to these rules, and one draw needn't show every extreme that they name: `recv_dest`: on each receiving device the used values are distinct rows; from one sending device at most 2 slots are used, and one device of each grid uses every slot.
All inputs are finite; a program needn't handle non-finite values.
Results may differ from the reference program's by a relative error of at most 0.00002.
Values sent between devices are 32-bit elements; how exact they have to be, the bound alone decides.
No kernel may reach another device: no remote copies, remote signals or barrier semaphores. Data moves between devices by JAX's collectives and lax.ppermute only.
A program may use at most 64 MiB of HBM per device.

```python
import math
import jax
import jax.numpy as jnp
from jax import lax

CELLS_FIRST_DIM = 8
CELLS_SECOND_DIM = 32
CELLS_THIRD_DIM = 256
ROW_LENGTH = 128
CAP = 2
OVERSET_GRIDS = 2
GRID_DEVICES = 128
BLOCK_ROWS = 512
NX = 128
NY = 256
N_STREAM = 16
N_SPAN = 8


def draw_recv_dest(key, part):
    total = OVERSET_GRIDS * GRID_DEVICES
    device_keys = jax.random.split(jax.random.fold_in(key, 11), total)
    full = jax.random.randint(jax.random.fold_in(key, 12), (OVERSET_GRIDS,), 0, GRID_DEVICES)

    def one_device(device_key, index):
        count_key, order_key = jax.random.split(device_key)
        counts = jax.random.randint(count_key, (GRID_DEVICES,), 0, CAP + 1)
        grid_index = index // GRID_DEVICES
        peer_index = index % GRID_DEVICES
        counts = jnp.where(full[grid_index] == peer_index, CAP, counts)
        slots = jnp.arange(CAP, dtype=jnp.int32)
        used = (slots[None, :] < counts[:, None]).reshape(-1)
        ranks = jnp.cumsum(used.astype(jnp.int32)) - 1
        order = jax.random.permutation(order_key, BLOCK_ROWS)
        chosen = order[jnp.clip(ranks, 0, BLOCK_ROWS - 1)]
        return jnp.where(used, chosen, BLOCK_ROWS).reshape(GRID_DEVICES, CAP)
    result = jax.vmap(one_device)(device_keys, jnp.arange(total, dtype=jnp.int32))
    return result.reshape(OVERSET_GRIDS, N_STREAM, N_SPAN, GRID_DEVICES, CAP).astype(jnp.int32)


def touch_ends(entries, own_key, least, largest):
    spot = [jax.random.randint(jax.random.fold_in(own_key, axis), (), 0, length) for axis, length in enumerate(entries.shape)]
    main_axis = entries.shape.index(max(entries.shape))
    next_to = spot[:main_axis] + [(spot[main_axis] + 1) % entries.shape[main_axis]] + spot[main_axis + 1:]
    return entries.at[tuple(spot)].set(least).at[tuple(next_to)].set(largest)


def levels(rng, shape, cuts, low, largest):
    level, own = 1.0, jax.random.fold_in(rng, 6)
    for axis_at, parts in cuts:
        heights = jnp.exp(jax.random.uniform(jax.random.fold_in(own, axis_at), (parts,), jnp.float32, low / len(cuts), largest / len(cuts)))
        level = level * jnp.repeat(heights, shape[axis_at] // parts).reshape([-1 if axis == axis_at else 1 for axis in range(len(shape))])
    return level


def normal_values(key, extent, spread, reach, pieces=(), kind=jnp.bfloat16):
    drawn = jax.random.normal(key, extent, jnp.float32) * spread
    if len(pieces) > 0:
        drawn = levels(key, extent, pieces, -0.22, 0.18) * drawn
    return jnp.clip(drawn, min=-reach, max=reach).astype(kind)


def setup_inputs(seed: int = 0) -> dict:
    key_of = jax.random.split(jax.random.key(seed), 6)
    velocity = normal_values(key_of[0], (3, OVERSET_GRIDS, NX, NY, CELLS_THIRD_DIM), 0.8, 2.5, ((1, 2), (2, 16), (3, 8)), jnp.float32)
    history = jnp.clip(jnp.exp(math.log(10.0) - 4.6051702 * jax.random.uniform(key_of[1], (2, OVERSET_GRIDS, NX, NY, CELLS_THIRD_DIM), jnp.float32) ** levels(key_of[1], (2, OVERSET_GRIDS, NX, NY, CELLS_THIRD_DIM), ((1, 2), (2, 16), (3, 8)), -0.2, 0.2)), 0.1, 10.0)
    donor_rows = touch_ends(jax.random.randint(key_of[2], (OVERSET_GRIDS, N_STREAM, N_SPAN, GRID_DEVICES, CAP, 2), 0, BLOCK_ROWS), jax.random.fold_in(key_of[2], 1), 0, BLOCK_ROWS - 1).astype(jnp.int32)
    recv_dest = draw_recv_dest(jax.random.fold_in(key_of[5], 71), 0)
    recv_weight = jnp.clip(1.0 * jax.random.uniform(key_of[4], (OVERSET_GRIDS, N_STREAM, N_SPAN, GRID_DEVICES, CAP), jnp.float32) ** levels(key_of[4], (OVERSET_GRIDS, N_STREAM, N_SPAN, GRID_DEVICES, CAP), ((0, 2), (1, 16), (2, 8)), -0.2, 0.2), 0.0, 1.0)
    return {"velocity": velocity, "history": history, "donor_rows": donor_rows, "recv_dest": recv_dest, "recv_weight": recv_weight}


step_time = 0.2

def cut(scalar_field, start, stop, axis):
    return lax.slice_in_dim(scalar_field, start, stop, axis=axis)

def smooth_axis(scalar_field, axis):
    size = scalar_field.shape[axis]
    return 0.25 * (cut(scalar_field, 0, size - 2, axis) + cut(scalar_field, 2, size, axis)) + 0.5 * cut(scalar_field, 1, size - 1, axis)

def slope_axis(scalar_field, axis):
    size = scalar_field.shape[axis]
    return 0.5 * (cut(scalar_field, 2, size, axis) - cut(scalar_field, 0, size - 2, axis))

def box_valid(scalar_field):
    return smooth_axis(smooth_axis(smooth_axis(scalar_field, 1), 2), 3)

def pad_space(scalar_field):
    return jnp.pad(scalar_field, ((0, 0), (1, 1), (1, 1), (1, 1)))

def strain_from(vel):
    grad_x = slope_axis(vel[:, :, 1:-1, 1:-1], 1)
    grad_y = slope_axis(vel[:, 1:-1, :, 1:-1], 2)
    grad_z = slope_axis(vel[:, 1:-1, 1:-1, :], 3)
    return jnp.stack([grad_x[0], grad_y[1], grad_z[2], 0.5 * (grad_y[0] + grad_x[1]), 0.5 * (grad_z[0] + grad_x[2]), 0.5 * (grad_z[1] + grad_y[2])])

def magnitude(tensor):
    return jnp.sqrt(2.0 * (tensor[0] * tensor[0] + tensor[1] * tensor[1] + tensor[2] * tensor[2] + 2.0 * (tensor[3] * tensor[3] + tensor[4] * tensor[4] + tensor[5] * tensor[5])))

def pairs(vel):
    return jnp.stack([vel[0] * vel[0], vel[1] * vel[1], vel[2] * vel[2], vel[0] * vel[1], vel[0] * vel[2], vel[1] * vel[2]])

def contract(left, right):
    return left[0] * right[0] + left[1] * right[1] + left[2] * right[2] + 2.0 * (left[3] * right[3] + left[4] * right[4] + left[5] * right[5])

def carry_axis(scalar_field, speed, axis):
    size = scalar_field.shape[axis]
    lower = cut(scalar_field, 0, size - 2, axis)
    middle = cut(scalar_field, 1, size - 1, axis)
    upper = cut(scalar_field, 2, size, axis)
    return middle + jnp.maximum(speed, 0.0) * (lower - middle) + jnp.maximum(-speed, 0.0) * (upper - middle)

def close_model(vel_pad, lagr_pad, s_hat, ms_hat):
    u_hat = box_valid(vel_pad)
    uu_hat = box_valid(pairs(vel_pad))
    lterm = uu_hat - pairs(u_hat)
    mterm = 2.0 * (ms_hat - 4.0 * magnitude(s_hat) * s_hat)
    lm_term = contract(lterm, mterm)
    mm_term = contract(mterm, mterm)
    speed = step_time * vel_pad
    moved = carry_axis(lagr_pad, speed[0, 1:-1], 1)
    moved = carry_axis(moved, speed[1, 1:-1, 1:-1], 2)
    moved = carry_axis(moved, speed[2, 1:-1, 1:-1, 1:-1], 3)
    rate = step_time / 1.5 * (moved[0] * moved[1]) ** 0.125
    blend = rate / (1.0 + rate)
    new_lm = jnp.maximum(blend * lm_term + (1.0 - blend) * moved[0], 0.0)
    new_mm = blend * mm_term + (1.0 - blend) * moved[1]
    return jnp.stack([new_lm, new_mm])

def one_grid(pair):
    vel, lagr = pair
    vel_pad = pad_space(vel)
    strain = strain_from(vel_pad)
    mag = magnitude(strain)
    product = mag * strain
    s_hat = box_valid(pad_space(strain))
    ms_hat = box_valid(pad_space(product))
    return (close_model(vel_pad, pad_space(lagr), s_hat, ms_hat), mag)

def to_blocks(scalar_field):
    vertical_rows = CELLS_THIRD_DIM // ROW_LENGTH
    reshaped_field = scalar_field.reshape(OVERSET_GRIDS, 2, N_STREAM, CELLS_FIRST_DIM, N_SPAN, CELLS_SECOND_DIM, vertical_rows, ROW_LENGTH)
    return reshaped_field.transpose(0, 1, 2, 4, 3, 5, 6, 7).reshape(OVERSET_GRIDS, 2, GRID_DEVICES, BLOCK_ROWS, ROW_LENGTH)

def from_blocks(device_blocks):
    vertical_rows = CELLS_THIRD_DIM // ROW_LENGTH
    reshaped_field = device_blocks.reshape(OVERSET_GRIDS, 2, N_STREAM, N_SPAN, CELLS_FIRST_DIM, CELLS_SECOND_DIM, vertical_rows, ROW_LENGTH)
    return reshaped_field.transpose(0, 1, 2, 4, 3, 5, 6, 7).reshape(OVERSET_GRIDS, 2, NX, NY, CELLS_THIRD_DIM)

def pick(device_block, rows):
    return jnp.take(device_block, rows, axis=1)

def place(device_block, cell_values, target_cells):
    return device_block.at[:, target_cells.reshape(-1)].set(cell_values.reshape(2, -1, ROW_LENGTH), mode='drop')

def reference(velocity, history, donor_rows, recv_dest, recv_weight):
    updated_field, mag = lax.map(one_grid, (jnp.moveaxis(velocity, 1, 0), jnp.moveaxis(history, 1, 0)))
    retained_values = to_blocks(jnp.moveaxis(history, 1, 0))
    donors = donor_rows.reshape(OVERSET_GRIDS, GRID_DEVICES, GRID_DEVICES, CAP, 2)
    picked = jax.vmap(jax.vmap(pick, in_axes=(1, 0)), in_axes=(0, 0))(retained_values, donors)
    received = picked[::-1].transpose(0, 3, 2, 1, 4, 5, 6)
    weight = recv_weight.reshape(OVERSET_GRIDS, GRID_DEVICES, GRID_DEVICES, CAP)[:, :, None, :, :, None]
    blended_values = weight * received[..., 0, :] + (1.0 - weight) * received[..., 1, :]
    device_blocks = to_blocks(updated_field).transpose(0, 2, 1, 3, 4)
    dests = recv_dest.reshape(OVERSET_GRIDS, GRID_DEVICES, GRID_DEVICES, CAP)
    device_blocks = jax.vmap(jax.vmap(place))(device_blocks, blended_values, dests)
    final = from_blocks(device_blocks.transpose(0, 2, 1, 3, 4))
    eddy = final[:, 0] / final[:, 1] * mag
    return (jnp.moveaxis(final, 0, 1), eddy)
```

```python
import jax
import jax.numpy as jnp
from jax import lax
from jax.experimental import pallas as pl
from jax.experimental.pallas import tpu as pltpu
from jax.sharding import PartitionSpec as P

F32 = jnp.float32
BF16 = jnp.bfloat16
NXL, NYL, NZ, ROW = 8, 32, 256, 128
ROWS = 512
PEERS = 128
CAP = 2
EXT = 40
DT = 0.2
VMEM_LIMIT = 56 * 1024 * 1024
PAIRS = ((0, 0), (1, 1), (2, 2), (0, 1), (0, 2), (1, 2))


def params():
    return pltpu.CompilerParams(vmem_limit_bytes=VMEM_LIMIT)


def shift_ring(x, axis, step):
    n = lax.axis_size(axis)
    return lax.ppermute(x, axis, [(i, (i + step) % n) for i in range(n)])


def split3(x):
    hi = x.astype(BF16)
    rest = x - hi.astype(F32)
    mid = rest.astype(BF16)
    low = (rest - mid.astype(F32)).astype(BF16)
    return hi, mid, low


def exact_dot(onehot, x):
    hi, mid, low = split3(x)
    out = jnp.dot(onehot, hi, preferred_element_type=F32)
    out = out + jnp.dot(onehot, mid, preferred_element_type=F32)
    return out + jnp.dot(onehot, low, preferred_element_type=F32)


def gather_kernel(hist_ref, idx_ref, out_ref):
    halves = []
    for h in range(2):
        cols = [
            hist_ref[f, :, :, h * ROW : (h + 1) * ROW].reshape(NXL * NYL, ROW)
            for f in range(2)
        ]
        halves.append(split3(jnp.concatenate(cols, axis=1)))
    idx = idx_ref[...]
    place = (idx % 2) * (ROWS // 2) + idx // 2
    place = jnp.transpose(jnp.concatenate([place, place], axis=0).astype(F32))
    lanes = lax.broadcasted_iota(jnp.int32, (PEERS, ROWS // 2), 1).astype(F32)
    for j in range(2 * CAP):
        col = place[:, j : j + 1]
        acc = None
        for h in range(2):
            onehot = jnp.where(lanes + float(h * ROWS // 2) == col, 1.0, 0.0).astype(BF16)
            for part in halves[h]:
                d = jnp.dot(onehot, part, preferred_element_type=F32)
                acc = d if acc is None else acc + d
        for f in range(2):
            out_ref[:, f * 4 + j, :] = acc[:, f * ROW : (f + 1) * ROW]


def gather(hist, idx):
    return pl.pallas_call(
        gather_kernel,
        out_shape=jax.ShapeDtypeStruct((PEERS, 8, ROW), F32),
        compiler_params=params(),
        name="pick_donors",
        cost_estimate=pl.CostEstimate(
            flops=400_000_000, transcendentals=0, bytes_accessed=1_100_000
        ),
    )(hist, idx)


def edge_kernel(vel_lo, vel_hi, his_lo, his_hi, xl_ref, xr_ref, up_ref, down_ref):
    b = lax.axis_index("span")
    last = lax.axis_size("span") - 1
    keep_up = jnp.where(b == last, 0.0, 1.0)
    keep_down = jnp.where(b == 0, 0.0, 1.0)
    for layer in range(12):
        for c in range(3):
            if layer < 2:
                top, bot = xl_ref[c * 2 + layer, 30:32, :], xl_ref[c * 2 + layer, 0:2, :]
            elif layer < 10:
                top, bot = vel_hi[c, layer - 2, 6:8, :], vel_lo[c, layer - 2, 0:2, :]
            else:
                top = xr_ref[c * 2 + layer - 10, 30:32, :]
                bot = xr_ref[c * 2 + layer - 10, 0:2, :]
            up_ref[layer, c * 2 : c * 2 + 2, :] = top * keep_up
            down_ref[layer, c * 2 : c * 2 + 2, :] = bot * keep_down
        for f in range(2):
            if layer in (0, 11):
                top = bot = jnp.zeros((1, NZ), F32)
            elif layer == 1:
                top, bot = xl_ref[6 + f, 31:32, :], xl_ref[6 + f, 0:1, :]
            elif layer == 10:
                top, bot = xr_ref[6 + f, 31:32, :], xr_ref[6 + f, 0:1, :]
            else:
                top, bot = his_hi[f, layer - 2, 7:8, :], his_lo[f, layer - 2, 0:1, :]
            up_ref[layer, 6 + f : 7 + f, :] = top * keep_up
            down_ref[layer, 6 + f : 7 + f, :] = bot * keep_down


def edges(vel, hist, xl, xr):
    def rows(n, tile):
        return pl.BlockSpec((n, NXL, 8, NZ), lambda i: (0, 0, tile, 0))

    whole = pl.BlockSpec((8, NYL, NZ), lambda i: (0, 0, 0))
    out = pl.BlockSpec((12, 8, NZ), lambda i: (0, 0, 0))
    shape = jax.ShapeDtypeStruct((12, 8, NZ), F32)
    return pl.pallas_call(
        edge_kernel,
        grid=(1,),
        in_specs=[rows(3, 0), rows(3, 3), rows(2, 0), rows(2, 3), whole, whole],
        out_specs=[out, out],
        out_shape=[shape, shape],
        compiler_params=params(),
        name="edge_rows",
        cost_estimate=pl.CostEstimate(flops=100_000, transcendentals=0, bytes_accessed=1_000_000),
    )(vel, vel, hist, hist, xl, xr)


def add(a, b):
    return tuple(p + q for p, q in zip(a, b))


def sub(a, b):
    return tuple(p - q for p, q in zip(a, b))


def mul(a, b):
    return tuple(p * q for p, q in zip(a, b))


def each(fn, *a):
    return tuple(fn(*p) for p in zip(*a))


def y_next(a):
    return tuple(pltpu.roll(p, EXT - 1, 0) for p in a)


def y_prev(a):
    return tuple(pltpu.roll(p, 1, 0) for p in a)


def own(a):
    return tuple(p[:NYL] for p in a)


def z_prev(a, first, fill):
    lo, hi = a
    rlo, rhi = pltpu.roll(lo, 1, 1), pltpu.roll(hi, 1, 1)
    m = first[: lo.shape[0]]
    return jnp.where(m, fill, rlo), jnp.where(m, rlo, rhi)


def z_next(a, last, fill):
    lo, hi = a
    rlo, rhi = pltpu.roll(lo, ROW - 1, 1), pltpu.roll(hi, ROW - 1, 1)
    m = last[: lo.shape[0]]
    return jnp.where(m, rhi, rlo), jnp.where(m, fill, rhi)


def stencil_kernel(
    vel_ref, his_ref, xl_ref, xr_ref, below_ref, above_ref, new_ref, mag_ref, v_ref, h_ref, s_ref
):
    a_id = lax.axis_index("stream")
    b_id = lax.axis_index("span")
    a_last = lax.axis_size("stream") - 1
    b_last = lax.axis_size("span") - 1
    halves = (slice(0, ROW), slice(ROW, NZ))

    zero4 = jnp.zeros((4, ROW), F32)
    for z, cols in enumerate(halves):
        for c in range(3):
            for layer in range(12):
                if layer < 2:
                    v_ref[c, layer, z, :NYL, :] = xl_ref[c * 2 + layer, :, cols]
                elif layer < 10:
                    v_ref[c, layer, z, :NYL, :] = vel_ref[c, layer - 2, :, cols]
                else:
                    v_ref[c, layer, z, :NYL, :] = xr_ref[c * 2 + layer - 10, :, cols]
                v_ref[c, layer, z, 32:34, :] = above_ref[layer, c * 2 : c * 2 + 2, cols]
                v_ref[c, layer, z, 34:38, :] = zero4
                v_ref[c, layer, z, 38:40, :] = below_ref[layer, c * 2 : c * 2 + 2, cols]
        for f in range(2):
            for layer in range(10):
                if layer == 0:
                    h_ref[f, layer, z, :NYL, :] = xl_ref[6 + f, :, cols]
                elif layer < 9:
                    h_ref[f, layer, z, :NYL, :] = his_ref[f, layer - 1, :, cols]
                else:
                    h_ref[f, layer, z, :NYL, :] = xr_ref[6 + f, :, cols]
                h_ref[f, layer, z, 32:33, :] = above_ref[layer + 1, 6 + f : 7 + f, cols]
                h_ref[f, layer, z, 33:37, :] = zero4
                h_ref[f, layer, z, 37:39, :] = zero4[:2]
                h_ref[f, layer, z, 39:40, :] = below_ref[layer + 1, 6 + f : 7 + f, cols]

    lane = lax.broadcasted_iota(jnp.int32, (EXT, ROW), 1)
    first, last = lane == 0, lane == ROW - 1
    row = lax.broadcasted_iota(jnp.int32, (EXT, ROW), 0)
    inside = jnp.where((row == 32) & (b_id == b_last), 0.0, 1.0) * jnp.where(
        (row == 39) & (b_id == 0), 0.0, 1.0
    )

    def get(ref, c, layer):
        return ref[c, layer, 0], ref[c, layer, 1]

    def smooth(below, mid, above):
        t = add(add(below, mid), add(mid, above))
        t = add(t, y_next(t))
        t = own(add(t, y_prev(t)))
        return add(add(t, t), add(z_prev(t, first, 0.0), z_next(t, last, 0.0)))

    def strain_layer(i, _):
        u = [get(v_ref, c, i + 1) for c in range(3)]
        keep = jnp.where(((i == 0) & (a_id == 0)) | ((i == 9) & (a_id == a_last)), 0.0, 1.0)
        m = inside * keep
        gx = [sub(get(v_ref, c, i + 2), get(v_ref, c, i)) for c in range(3)]
        gy = [sub(y_next(p), y_prev(p)) for p in u]
        gz = [sub(z_next(p, last, 0.0), z_prev(p, first, 0.0)) for p in u]
        t = [
            add(gx[0], gx[0]),
            add(gy[1], gy[1]),
            add(gz[2], gz[2]),
            add(gy[0], gx[1]),
            add(gz[0], gx[2]),
            add(gz[1], gy[2]),
        ]
        t = [each(lambda p: p * m, p) for p in t]
        q = [mul(p, p) for p in t]
        diag = add(add(q[0], q[1]), q[2])
        off = add(add(q[3], q[4]), q[5])
        mag = each(lambda p, r: jnp.sqrt((p + 2.0 * r) * 0.125), diag, off)

        @pl.when((i >= 1) & (i <= 8))
        def _():
            for z, cols in enumerate(halves):
                mag_ref[i - 1, :, cols] = mag[z][:NYL]

        for c in range(6):
            w = mul(mag, t[c])
            uu = mul(u[PAIRS[c][0]], u[PAIRS[c][1]])
            for z in range(2):
                s_ref[c, i, z] = t[c][z]
                s_ref[6 + c, i, z] = w[z]
                s_ref[12 + c, i, z] = uu[z]
        return 0

    lax.fori_loop(0, 10, strain_layer, 0)

    def close_layer(x, _):
        def hat(ref, c, at):
            return smooth(get(ref, c, at), get(ref, c, at + 1), get(ref, c, at + 2))

        s = [hat(s_ref, c, x) for c in range(6)]
        q = [mul(p, p) for p in s]
        diag = add(add(q[0], q[1]), q[2])
        off = add(add(q[3], q[4]), q[5])
        smag4 = each(lambda p, r: jnp.sqrt((p + 2.0 * r) * 0.125) * (4.0 / 64.0), diag, off)
        uh = [each(lambda p: p * (1.0 / 64.0), hat(v_ref, c, x + 1)) for c in range(3)]
        lm = mm = None
        for c in range(6):
            ms = hat(s_ref, 6 + c, x)
            m = each(lambda p, r, g: (p - g * r) * (1.0 / 128.0), ms, s[c], smag4)
            uu = hat(s_ref, 12 + c, x)
            ll = each(
                lambda p, r, g: p * (1.0 / 64.0) - r * g, uu, uh[PAIRS[c][0]], uh[PAIRS[c][1]]
            )
            m2 = m if c < 3 else add(m, m)
            dl, dm = mul(ll, m2), mul(m, m2)
            lm = dl if lm is None else add(lm, dl)
            mm = dm if mm is None else add(mm, dm)

        speed = [each(lambda p: DT * p, get(v_ref, c, x + 2)) for c in range(3)]
        moved = []
        for f in range(2):
            g = get(h_ref, f, x + 1)
            lower, upper = get(h_ref, f, x), get(h_ref, f, x + 2)

            def carry(mid, low, up, sp):
                return each(
                    lambda p, lo, hi, v: p + jnp.abs(v) * (jnp.where(v > 0, lo, hi) - p),
                    mid, low, up, sp,
                )

            g = carry(g, lower, upper, speed[0])
            g = carry(own(g), own(y_prev(g)), own(y_next(g)), own(speed[1]))
            g = carry(g, z_prev(g, first, 0.0), z_next(g, last, 0.0), own(speed[2]))
            moved.append(g)
        k = DT / 1.5
        for z, cols in enumerate(halves):
            m0, m1 = moved[0][z], moved[1][z]
            r = lax.rsqrt(lax.rsqrt(lax.rsqrt(m0 * m1)))
            blend = k / (r + k)
            new_ref[0, x, :, cols] = jnp.maximum(m0 + blend * (lm[z] - m0), 0.0)
            new_ref[1, x, :, cols] = m1 + blend * (mm[z] - m1)
        return 0

    lax.fori_loop(0, NXL, close_layer, 0)


def stencil(vel, hist, xl, xr, below, above):
    return pl.pallas_call(
        stencil_kernel,
        out_shape=[
            jax.ShapeDtypeStruct((2, NXL, NYL, NZ), F32),
            jax.ShapeDtypeStruct((NXL, NYL, NZ), F32),
        ],
        scratch_shapes=[
            pltpu.VMEM((3, 12, 2, EXT, ROW), F32),
            pltpu.VMEM((2, 10, 2, EXT, ROW), F32),
            pltpu.VMEM((18, 10, 2, EXT, ROW), F32),
        ],
        compiler_params=params(),
        name="stencil",
        cost_estimate=pl.CostEstimate(
            flops=60_000_000, transcendentals=500_000, bytes_accessed=20_000_000
        ),
    )(vel, hist, xl, xr, below, above)


def place_kernel(new_ref, mag_ref, got_ref, dest_ref, w_ref, out_ref, eddy_ref):
    w = jnp.transpose(jnp.concatenate([w_ref[...]] * 4, axis=0))
    blended = []
    for c in range(CAP):
        wc = w[:, c : c + 1]
        cols = []
        for f in range(2):
            r0, r1 = got_ref[:, f * 4 + c * 2, :], got_ref[:, f * 4 + c * 2 + 1, :]
            cols.append(wc * r0 + (1.0 - wc) * r1)
        blended.append(jnp.concatenate(cols, axis=1))
    parts = split3(jnp.concatenate(blended, axis=0))
    ones = jnp.ones((CAP * PEERS, ROW), BF16)
    dest = dest_ref[...]
    place = jnp.where(dest >= ROWS, -1, (dest % 2) * (ROWS // 2) + dest // 2)
    place = jnp.concatenate([place[0:1], place[1:2]], axis=1)
    rows = lax.broadcasted_iota(jnp.int32, (ROWS // 2, CAP * PEERS), 0)
    for h in range(2):
        onehot = jnp.where(rows + h * (ROWS // 2) == place, 1.0, 0.0).astype(BF16)
        acc = None
        for part in parts:
            d = jnp.dot(onehot, part, preferred_element_type=F32)
            acc = d if acc is None else acc + d
        hit = jnp.dot(onehot, ones, preferred_element_type=F32) > 0.5
        cols = slice(h * ROW, (h + 1) * ROW)
        final = []
        for f in range(2):
            cur = new_ref[f, :, :, cols].reshape(NXL * NYL, ROW)
            val = jnp.where(hit, acc[:, f * ROW : (f + 1) * ROW], cur)
            out_ref[f, :, :, cols] = val.reshape(NXL, NYL, ROW)
            final.append(val)
        eddy = final[0] / final[1] * mag_ref[:, :, cols].reshape(NXL * NYL, ROW)
        eddy_ref[:, :, cols] = eddy.reshape(NXL, NYL, ROW)


def place_rows(new, mag, got, dest, weight):
    return pl.pallas_call(
        place_kernel,
        out_shape=[
            jax.ShapeDtypeStruct((2, NXL, NYL, NZ), F32),
            jax.ShapeDtypeStruct((NXL, NYL, NZ), F32),
        ],
        compiler_params=params(),
        name="place_receptors",
        cost_estimate=pl.CostEstimate(
            flops=300_000_000, transcendentals=100_000, bytes_accessed=2_500_000
        ),
    )(new, mag, got, dest, weight)


def body(velocity, history, donor_rows, recv_dest, recv_weight):
    vel, hist = velocity[:, 0], history[:, 0]
    a_id = lax.axis_index("stream")
    a_last = lax.axis_size("stream") - 1

    swap = [(0, 1), (1, 0)]
    idx = jnp.transpose(donor_rows[0, 0, 0], (1, 2, 0)).reshape(2 * CAP, PEERS)
    other = lax.ppermute(hist, "grid", swap)
    other_idx = lax.ppermute(idx.astype(F32), "grid", swap).astype(jnp.int32)

    def faces(v, h):
        return jnp.concatenate([v.reshape(6, NYL, NZ), h.reshape(2, NYL, NZ)], axis=0)

    right = jnp.where(a_id == a_last, 0.0, faces(vel[:, 6:8], hist[:, 7:8]))
    left = jnp.where(a_id == 0, 0.0, faces(vel[:, 0:2], hist[:, 0:1]))
    xl = shift_ring(right, "stream", 1)
    xr = shift_ring(left, "stream", -1)

    chosen = gather(other, other_idx)
    got = lax.all_to_all(chosen, ("stream", "span"), split_axis=0, concat_axis=0, tiled=True)

    up, down = edges(vel, hist, xl, xr)
    below = shift_ring(up, "span", 1)
    above = shift_ring(down, "span", -1)
    new, mag = stencil(vel, hist, xl, xr, below, above)

    dest = jnp.transpose(recv_dest[0, 0, 0])
    weight = jnp.transpose(recv_weight[0, 0, 0])
    final, eddy = place_rows(new, mag, got, dest, weight)
    return final[:, None], eddy[None]


def solution(mesh):
    in_specs = (
        P(None, "grid", "stream", "span", None),
        P(None, "grid", "stream", "span", None),
        P("grid", "stream", "span", None, None, None),
        P("grid", "stream", "span", None, None),
        P("grid", "stream", "span", None, None),
    )
    out_specs = (P(None, "grid", "stream", "span", None), P("grid", "stream", "span", None))
    return jax.shard_map(body, mesh=mesh, in_specs=in_specs, out_specs=out_specs, check_vma=False)
```

```python
import jax
import jax.numpy as jnp
from jax import lax
from jax.experimental import pallas as pl
from jax.experimental.pallas import tpu as pltpu
from jax.sharding import PartitionSpec as P

F32 = jnp.float32
BF16 = jnp.bfloat16
NXL, NYL, NZ, ROW = 8, 32, 256, 128
ROWS = 512
PEERS = 128
CAP = 2
FACE = 8 * NYL
STENCIL_COST = 10_000_000_000
EXT = 40
DT = 0.2
MIB = 1024 * 1024
PAIRS = ((0, 0), (1, 1), (2, 2), (0, 1), (0, 2), (1, 2))


def in_vmem(n):
    return [pl.BlockSpec(memory_space=pltpu.VMEM)] * n


def params(mib):
    return pltpu.CompilerParams(vmem_limit_bytes=mib * MIB)


def shift_ring(x, axis, step):
    n = lax.axis_size(axis)
    return lax.ppermute(x, axis, [(i, (i + step) % n) for i in range(n)])


def split3(x):
    hi = x.astype(BF16)
    rest = x - hi.astype(F32)
    mid = rest.astype(BF16)
    low = (rest - mid.astype(F32)).astype(BF16)
    return hi, mid, low


def exact_dot(onehot, x):
    hi, mid, low = split3(x)
    out = jnp.dot(onehot, hi, preferred_element_type=F32)
    out = out + jnp.dot(onehot, mid, preferred_element_type=F32)
    return out + jnp.dot(onehot, low, preferred_element_type=F32)


def gather_kernel(hist_ref, idx_hbm, out_ref, idx_ref, sem):
    copy = pltpu.make_async_copy(idx_hbm, idx_ref, sem)
    copy.start()
    halves = []
    for h in range(2):
        cols = [
            hist_ref[f, :, :, h * ROW : (h + 1) * ROW].reshape(NXL * NYL, ROW)
            for f in range(2)
        ]
        halves.append(split3(jnp.concatenate(cols, axis=1)))
    copy.wait()
    idx = idx_ref[...]
    place = (idx % 2) * (ROWS // 2) + idx // 2
    place = jnp.transpose(jnp.concatenate([place, place], axis=0).astype(F32))
    lanes = lax.broadcasted_iota(jnp.int32, (PEERS, ROWS // 2), 1).astype(F32)
    for j in range(2 * CAP):
        col = place[:, j : j + 1]
        acc = None
        for h in range(2):
            onehot = jnp.where(lanes + float(h * ROWS // 2) == col, 1.0, 0.0).astype(BF16)
            for part in halves[h]:
                d = jnp.dot(onehot, part, preferred_element_type=F32)
                acc = d if acc is None else acc + d
        for f in range(2):
            out_ref[:, f * 4 + j, :] = acc[:, f * ROW : (f + 1) * ROW]


def gather(hist, idx):
    return pl.pallas_call(
        gather_kernel,
        in_specs=in_vmem(1) + [pl.BlockSpec(memory_space=pl.ANY)],
        out_specs=in_vmem(1)[0],
        scratch_shapes=[
            pltpu.VMEM((2 * CAP, PEERS), jnp.int32),
            pltpu.SemaphoreType.DMA(()),
        ],
        out_shape=jax.ShapeDtypeStruct((PEERS, 8, ROW), F32),
        compiler_params=params(8),
        name="pick_donors",
        cost_estimate=pl.CostEstimate(
            flops=400_000_000, transcendentals=0, bytes_accessed=1_100_000
        ),
    )(hist, idx)


def edge_kernel(vel_ref, his_ref, up_ref, down_ref):
    b = lax.axis_index("span")
    last = lax.axis_size("span") - 1
    keep_up = jnp.where(b == last, 0.0, 1.0)
    keep_down = jnp.where(b == 0, 0.0, 1.0)
    for layer in range(NXL):
        for c in range(3):
            rows = slice(c * 2, c * 2 + 2)
            up_ref[layer, rows, :] = vel_ref[c, layer, NYL - 2 :, :] * keep_up
            down_ref[layer, rows, :] = vel_ref[c, layer, :2, :] * keep_down
        for f in range(2):
            rows = slice(6 + f, 7 + f)
            up_ref[layer, rows, :] = his_ref[f, layer, NYL - 1 :, :] * keep_up
            down_ref[layer, rows, :] = his_ref[f, layer, :1, :] * keep_down


def edges(vel, hist):
    shape = jax.ShapeDtypeStruct((NXL, 8, NZ), F32)
    return pl.pallas_call(
        edge_kernel,
        in_specs=in_vmem(2),
        out_specs=in_vmem(2),
        out_shape=[shape, shape],
        compiler_params=params(4),
        name="edge_rows",
        cost_estimate=pl.CostEstimate(flops=100_000, transcendentals=0, bytes_accessed=1_000_000),
    )(vel, hist)


def face_kernel(vel_ref, his_ref, below_ref, above_ref, right_ref, left_ref):
    a = lax.axis_index("stream")
    last = lax.axis_size("stream") - 1
    for out_ref, first, hist_layer, keep in (
        (right_ref, NXL - 2, NXL - 1, jnp.where(a == last, 0.0, 1.0)),
        (left_ref, 0, 0, jnp.where(a == 0, 0.0, 1.0)),
    ):
        for k in range(8):
            if k < 6:
                c, layer = k // 2, first + k % 2
                plane = vel_ref[c, layer]
                rows = slice(c * 2, c * 2 + 2)
                up, down = above_ref[layer, rows, :], below_ref[layer, rows, :]
            else:
                layer = hist_layer
                plane = his_ref[k - 6, layer]
                up, down = above_ref[layer, k : k + 1, :], below_ref[layer, k : k + 1, :]
            out_ref[k * NYL : (k + 1) * NYL, :] = plane * keep
            base, n = FACE + 4 * k, up.shape[0]
            out_ref[base : base + n, :] = up * keep
            out_ref[base + 4 - n : base + 4, :] = down * keep
            if n == 1:
                out_ref[base + 1 : base + 3, :] = jnp.zeros((2, NZ), F32)


def faces(vel, hist, below, above):
    shape = jax.ShapeDtypeStruct((FACE + 32, NZ), F32)
    return pl.pallas_call(
        face_kernel,
        in_specs=in_vmem(4),
        out_specs=in_vmem(2),
        out_shape=[shape, shape],
        compiler_params=params(4),
        name="face_layers",
        cost_estimate=pl.CostEstimate(flops=200_000, transcendentals=0, bytes_accessed=1_200_000),
    )(vel, hist, below, above)


def add(a, b):
    return tuple(p + q for p, q in zip(a, b))


def sub(a, b):
    return tuple(p - q for p, q in zip(a, b))


def mul(a, b):
    return tuple(p * q for p, q in zip(a, b))


def each(fn, *a):
    return tuple(fn(*p) for p in zip(*a))


def y_next(a):
    return tuple(pltpu.roll(p, EXT - 1, 0) for p in a)


def y_prev(a):
    return tuple(pltpu.roll(p, 1, 0) for p in a)


def own(a):
    return tuple(p[:NYL] for p in a)


def z_prev(a, first, fill):
    lo, hi = a
    rlo, rhi = pltpu.roll(lo, 1, 1), pltpu.roll(hi, 1, 1)
    m = first[: lo.shape[0]]
    return jnp.where(m, fill, rlo), jnp.where(m, rlo, rhi)


def z_next(a, last, fill):
    lo, hi = a
    rlo, rhi = pltpu.roll(lo, ROW - 1, 1), pltpu.roll(hi, ROW - 1, 1)
    m = last[: lo.shape[0]]
    return jnp.where(m, rhi, rlo), jnp.where(m, fill, rhi)


def placement(dest_ref, w_ref, table_ref):
    dest = dest_ref[...]
    place = jnp.where(dest >= ROWS, -1, (dest % 2) * (ROWS // 2) + dest // 2).astype(F32)
    for c in range(CAP):
        table_ref[c : c + 1, :] = place[c : c + 1]
    table_ref[8:, :] = jnp.zeros((PEERS, ROW), F32)
    table_ref[8:, 0:8] = jnp.transpose(jnp.concatenate([w_ref[...]] * 4, axis=0))


def stencil_kernel(
    vel_hbm, his_hbm, xl_hbm, xr_hbm, below_ref, above_ref, dest_hbm, w_hbm,
    new_ref, mag_ref, table_ref,
    v_ref, h_ref, s_ref, corner_ref, dest_ref, w_ref, sems,
):
    a_id = lax.axis_index("stream")
    b_id = lax.axis_index("span")
    a_last = lax.axis_size("stream") - 1
    b_last = lax.axis_size("span") - 1
    halves = (slice(0, ROW), slice(ROW, NZ))

    copies = [
        pltpu.make_async_copy(
            ref.at[pl.ds(FACE, 32), :], corner_ref.at[side], sems.at[side]
        )
        for side, ref in enumerate((xl_hbm, xr_hbm))
    ]
    copies.append(pltpu.make_async_copy(dest_hbm, dest_ref, sems.at[38]))
    copies.append(pltpu.make_async_copy(w_hbm, w_ref, sems.at[39]))
    for z, cols in enumerate(halves):
        lanes = pl.ds(z * ROW, ROW)
        copies.append(
            pltpu.make_async_copy(
                vel_hbm.at[:, :, :, lanes],
                v_ref.at[:, pl.ds(2, NXL), z, pl.ds(0, NYL), :],
                sems.at[2 + z],
            )
        )
        copies.append(
            pltpu.make_async_copy(
                his_hbm.at[:, :, :, lanes],
                h_ref.at[:, pl.ds(1, NXL), z, pl.ds(0, NYL), :],
                sems.at[4 + z],
            )
        )
        for side, ref in enumerate((xl_hbm, xr_hbm)):
            for k in range(8):
                rows = pl.ds(k * NYL, NYL)
                if k < 6:
                    to = v_ref.at[k // 2, side * 10 + k % 2, z, pl.ds(0, NYL), :]
                else:
                    to = h_ref.at[k - 6, side * 9, z, pl.ds(0, NYL), :]
                copies.append(
                    pltpu.make_async_copy(
                        ref.at[rows, lanes], to, sems.at[6 + (side * 2 + z) * 8 + k]
                    )
                )
    for copy in copies:
        copy.start()

    zero4 = jnp.zeros((4, ROW), F32)

    def fill(ref, c, layer, z, up, down):
        n = up.shape[0]
        ref[c, layer, z, NYL : NYL + n, :] = up
        ref[c, layer, z, NYL + n : NYL + n + 4, :] = zero4
        ref[c, layer, z, NYL + 4 : EXT - n, :] = zero4[: 4 - n]
        ref[c, layer, z, EXT - n :, :] = down

    for z, cols in enumerate(halves):
        for layer in range(NXL):
            for c in range(3):
                rows = slice(c * 2, c * 2 + 2)
                up, down = above_ref[layer, rows, cols], below_ref[layer, rows, cols]
                fill(v_ref, c, layer + 2, z, up, down)
            for f in range(2):
                rows = slice(6 + f, 7 + f)
                up, down = above_ref[layer, rows, cols], below_ref[layer, rows, cols]
                fill(h_ref, f, layer + 1, z, up, down)
    for copy in copies:
        copy.wait()
    placement(dest_ref, w_ref, table_ref)
    for z, cols in enumerate(halves):
        for side in range(2):
            for k in range(8):
                n = 2 if k < 6 else 1
                up = corner_ref[side, 4 * k : 4 * k + n, cols]
                down = corner_ref[side, 4 * k + 4 - n : 4 * k + 4, cols]
                if k < 6:
                    fill(v_ref, k // 2, side * 10 + k % 2, z, up, down)
                else:
                    fill(h_ref, k - 6, side * 9, z, up, down)

    lane = lax.broadcasted_iota(jnp.int32, (EXT, ROW), 1)
    first, last = lane == 0, lane == ROW - 1
    row = lax.broadcasted_iota(jnp.int32, (EXT, ROW), 0)
    inside = jnp.where((row == 32) & (b_id == b_last), 0.0, 1.0) * jnp.where(
        (row == 39) & (b_id == 0), 0.0, 1.0
    )

    def get(ref, c, layer):
        return ref[c, layer, 0], ref[c, layer, 1]

    def smooth(below, mid, above):
        t = add(add(below, mid), add(mid, above))
        t = add(t, y_next(t))
        t = own(add(t, y_prev(t)))
        return add(add(t, t), add(z_prev(t, first, 0.0), z_next(t, last, 0.0)))

    def strain_layer(i, _):
        u = [get(v_ref, c, i + 1) for c in range(3)]
        keep = jnp.where(((i == 0) & (a_id == 0)) | ((i == 9) & (a_id == a_last)), 0.0, 1.0)
        m = inside * keep
        gx = [sub(get(v_ref, c, i + 2), get(v_ref, c, i)) for c in range(3)]
        gy = [sub(y_next(p), y_prev(p)) for p in u]
        gz = [sub(z_next(p, last, 0.0), z_prev(p, first, 0.0)) for p in u]
        t = [
            add(gx[0], gx[0]),
            add(gy[1], gy[1]),
            add(gz[2], gz[2]),
            add(gy[0], gx[1]),
            add(gz[0], gx[2]),
            add(gz[1], gy[2]),
        ]
        t = [each(lambda p: p * m, p) for p in t]
        q = [mul(p, p) for p in t]
        diag = add(add(q[0], q[1]), q[2])
        off = add(add(q[3], q[4]), q[5])
        mag = each(lambda p, r: jnp.sqrt((p + 2.0 * r) * 0.125), diag, off)

        @pl.when((i >= 1) & (i <= 8))
        def _():
            for z, cols in enumerate(halves):
                mag_ref[i - 1, :, cols] = mag[z][:NYL]

        for c in range(6):
            w = mul(mag, t[c])
            uu = mul(u[PAIRS[c][0]], u[PAIRS[c][1]])
            for z in range(2):
                s_ref[c, i, z] = t[c][z]
                s_ref[6 + c, i, z] = w[z]
                s_ref[12 + c, i, z] = uu[z]
        return 0

    lax.fori_loop(0, 10, strain_layer, 0)

    def close_layer(x, _):
        def hat(ref, c, at):
            return smooth(get(ref, c, at), get(ref, c, at + 1), get(ref, c, at + 2))

        s = [hat(s_ref, c, x) for c in range(6)]
        q = [mul(p, p) for p in s]
        diag = add(add(q[0], q[1]), q[2])
        off = add(add(q[3], q[4]), q[5])
        smag4 = each(lambda p, r: jnp.sqrt((p + 2.0 * r) * 0.125) * (4.0 / 64.0), diag, off)
        uh = [each(lambda p: p * (1.0 / 64.0), hat(v_ref, c, x + 1)) for c in range(3)]
        lm = mm = None
        for c in range(6):
            ms = hat(s_ref, 6 + c, x)
            m = each(lambda p, r, g: (p - g * r) * (1.0 / 128.0), ms, s[c], smag4)
            uu = hat(s_ref, 12 + c, x)
            ll = each(
                lambda p, r, g: p * (1.0 / 64.0) - r * g, uu, uh[PAIRS[c][0]], uh[PAIRS[c][1]]
            )
            m2 = m if c < 3 else add(m, m)
            dl, dm = mul(ll, m2), mul(m, m2)
            lm = dl if lm is None else add(lm, dl)
            mm = dm if mm is None else add(mm, dm)

        speed = [each(lambda p: DT * p, get(v_ref, c, x + 2)) for c in range(3)]
        moved = []
        for f in range(2):
            g = get(h_ref, f, x + 1)
            lower, upper = get(h_ref, f, x), get(h_ref, f, x + 2)

            def carry(mid, low, up, sp):
                return each(
                    lambda p, lo, hi, v: p + jnp.abs(v) * (jnp.where(v > 0, lo, hi) - p),
                    mid, low, up, sp,
                )

            g = carry(g, lower, upper, speed[0])
            g = carry(own(g), own(y_prev(g)), own(y_next(g)), own(speed[1]))
            g = carry(g, z_prev(g, first, 0.0), z_next(g, last, 0.0), own(speed[2]))
            moved.append(g)
        k = DT / 1.5
        for z, cols in enumerate(halves):
            m0, m1 = moved[0][z], moved[1][z]
            r = lax.rsqrt(lax.rsqrt(lax.rsqrt(m0 * m1)))
            blend = k / (r + k)
            new_ref[0, x, :, cols] = jnp.maximum(m0 + blend * (lm[z] - m0), 0.0)
            new_ref[1, x, :, cols] = m1 + blend * (mm[z] - m1)
        return 0

    lax.fori_loop(0, NXL, close_layer, 0)


def stencil(vel, hist, xl, xr, below, above, dest, weight):
    return pl.pallas_call(
        stencil_kernel,
        in_specs=[pl.BlockSpec(memory_space=pl.ANY)] * 4 + in_vmem(2) + [pl.BlockSpec(memory_space=pl.ANY)] * 2,
        out_specs=in_vmem(3),
        out_shape=[
            jax.ShapeDtypeStruct((2, NXL, NYL, NZ), F32),
            jax.ShapeDtypeStruct((NXL, NYL, NZ), F32),
            jax.ShapeDtypeStruct((8 + PEERS, ROW), F32),
        ],
        scratch_shapes=[
            pltpu.VMEM((3, 12, 2, EXT, ROW), F32),
            pltpu.VMEM((2, 10, 2, EXT, ROW), F32),
            pltpu.VMEM((18, 10, 2, EXT, ROW), F32),
            pltpu.VMEM((2, 32, NZ), F32),
            pltpu.VMEM((CAP, PEERS), jnp.int32),
            pltpu.VMEM((CAP, PEERS), F32),
            pltpu.SemaphoreType.DMA((40,)),
        ],
        compiler_params=params(16),
        name="stencil",
        cost_estimate=pl.CostEstimate(
            flops=STENCIL_COST, transcendentals=500_000, bytes_accessed=20_000_000
        ),
    )(vel, hist, xl, xr, below, above, dest, weight)


def place_kernel(new_ref, mag_ref, table_ref, got_ref, out_ref, eddy_ref):
    ones = jnp.ones((CAP * PEERS, ROW), BF16)
    place = jnp.concatenate([table_ref[0:1, :], table_ref[1:2, :]], axis=1)
    rows = lax.broadcasted_iota(jnp.int32, (ROWS // 2, CAP * PEERS), 0).astype(F32)
    blended = []
    for c in range(CAP):
        wc = table_ref[8:, c : c + 1]
        cols = []
        for f in range(2):
            r0, r1 = got_ref[:, f * 4 + c * 2, :], got_ref[:, f * 4 + c * 2 + 1, :]
            cols.append(wc * r0 + (1.0 - wc) * r1)
        blended.append(jnp.concatenate(cols, axis=1))
    parts = split3(jnp.concatenate(blended, axis=0))
    for h in range(2):
        onehot = jnp.where(rows + float(h * ROWS // 2) == place, 1.0, 0.0).astype(BF16)
        acc = None
        for part in parts:
            d = jnp.dot(onehot, part, preferred_element_type=F32)
            acc = d if acc is None else acc + d
        hit = jnp.dot(onehot, ones, preferred_element_type=F32) > 0.5
        cols = slice(h * ROW, (h + 1) * ROW)
        final = []
        for f in range(2):
            cur = new_ref[f, :, :, cols].reshape(NXL * NYL, ROW)
            val = jnp.where(hit, acc[:, f * ROW : (f + 1) * ROW], cur)
            out_ref[f, :, :, cols] = val.reshape(NXL, NYL, ROW)
            final.append(val)
        eddy = final[0] / final[1] * mag_ref[:, :, cols].reshape(NXL * NYL, ROW)
        eddy_ref[:, :, cols] = eddy.reshape(NXL, NYL, ROW)


def place_rows(new, mag, table, got):
    return pl.pallas_call(
        place_kernel,
        in_specs=in_vmem(4),
        out_specs=in_vmem(2),
        out_shape=[
            jax.ShapeDtypeStruct((2, NXL, NYL, NZ), F32),
            jax.ShapeDtypeStruct((NXL, NYL, NZ), F32),
        ],
        compiler_params=params(12),
        name="place_receptors",
        cost_estimate=pl.CostEstimate(
            flops=300_000_000, transcendentals=100_000, bytes_accessed=2_500_000
        ),
    )(new, mag, table, got)


def body(velocity, history, donor_rows, recv_dest, recv_weight):
    vel, hist = velocity[:, 0], history[:, 0]
    idx = jnp.transpose(donor_rows[0, 0, 0], (1, 2, 0)).reshape(2 * CAP, PEERS)

    up, down = edges(vel, hist)
    below = shift_ring(up, "span", 1)
    above = shift_ring(down, "span", -1)

    chosen = gather(hist, idx)
    chosen = lax.ppermute(chosen, "grid", [(0, 1), (1, 0)])
    got = lax.all_to_all(chosen, ("stream", "span"), split_axis=0, concat_axis=0, tiled=True)

    right, left = faces(vel, hist, below, above)
    xl = shift_ring(right, "stream", 1)
    xr = shift_ring(left, "stream", -1)
    dest = jnp.transpose(recv_dest[0, 0, 0])
    weight = jnp.transpose(recv_weight[0, 0, 0])
    made = stencil(vel, hist, xl, xr, below, above, dest, weight)
    final, eddy = place_rows(*made, got)
    return final[:, None], eddy[None]


def solution(mesh):
    in_specs = (
        P(None, "grid", "stream", "span", None),
        P(None, "grid", "stream", "span", None),
        P("grid", "stream", "span", None, None, None),
        P("grid", "stream", "span", None, None),
        P("grid", "stream", "span", None, None),
    )
    out_specs = (P(None, "grid", "stream", "span", None), P("grid", "stream", "span", None))
    return jax.shard_map(body, mesh=mesh, in_specs=in_specs, out_specs=out_specs, check_vma=False)
```

```python
import jax
import jax.numpy as jnp
from jax import lax
from jax.experimental import pallas as pl
from jax.experimental.pallas import tpu as pltpu
from jax.sharding import PartitionSpec as P

F32 = jnp.float32
BF16 = jnp.bfloat16
NXL, NYL, NZ, ROW = 8, 32, 256, 128
ROWS = 512
PEERS = 128
CAP = 2
FACE = 8 * NYL
EDGE_ROOM = 10500 * 1024
FACE_COST = 10_000_000_000
STENCIL_COST = 10_000_000_000
EXT = 40
DT = 0.2
MIB = 1024 * 1024
PAIRS = ((0, 0), (1, 1), (2, 2), (0, 1), (0, 2), (1, 2))


def in_vmem(n):
    return [pl.BlockSpec(memory_space=pltpu.VMEM)] * n


def params(mib):
    return pltpu.CompilerParams(vmem_limit_bytes=mib * MIB)


def shift_ring(x, axis, step):
    n = lax.axis_size(axis)
    return lax.ppermute(x, axis, [(i, (i + step) % n) for i in range(n)])


def split3(x):
    hi = x.astype(BF16)
    rest = x - hi.astype(F32)
    mid = rest.astype(BF16)
    low = (rest - mid.astype(F32)).astype(BF16)
    return hi, mid, low


def exact_dot(onehot, x):
    hi, mid, low = split3(x)
    out = jnp.dot(onehot, hi, preferred_element_type=F32)
    out = out + jnp.dot(onehot, mid, preferred_element_type=F32)
    return out + jnp.dot(onehot, low, preferred_element_type=F32)


def gather_kernel(hist_ref, idx_hbm, out_ref, idx_ref, sem):
    copy = pltpu.make_async_copy(idx_hbm, idx_ref, sem)
    copy.start()
    halves = []
    for h in range(2):
        cols = [
            hist_ref[f, :, :, h * ROW : (h + 1) * ROW].reshape(NXL * NYL, ROW)
            for f in range(2)
        ]
        halves.append(split3(jnp.concatenate(cols, axis=1)))
    copy.wait()
    idx = idx_ref[...]
    place = (idx % 2) * (ROWS // 2) + idx // 2
    place = jnp.transpose(jnp.concatenate([place, place], axis=0).astype(F32))
    lanes = lax.broadcasted_iota(jnp.int32, (PEERS, ROWS // 2), 1).astype(F32)
    for j in range(2 * CAP):
        col = place[:, j : j + 1]
        acc = None
        for h in range(2):
            onehot = jnp.where(lanes + float(h * ROWS // 2) == col, 1.0, 0.0).astype(BF16)
            for part in halves[h]:
                d = jnp.dot(onehot, part, preferred_element_type=F32)
                acc = d if acc is None else acc + d
        for f in range(2):
            out_ref[:, f * 4 + j, :] = acc[:, f * ROW : (f + 1) * ROW]


def gather(hist, idx):
    return pl.pallas_call(
        gather_kernel,
        in_specs=in_vmem(1) + [pl.BlockSpec(memory_space=pl.ANY)],
        out_specs=in_vmem(1)[0],
        scratch_shapes=[
            pltpu.VMEM((2 * CAP, PEERS), jnp.int32),
            pltpu.SemaphoreType.DMA(()),
        ],
        out_shape=jax.ShapeDtypeStruct((PEERS, 8, ROW), F32),
        compiler_params=params(8),
        name="pick_donors",
        cost_estimate=pl.CostEstimate(
            flops=400_000_000, transcendentals=0, bytes_accessed=1_100_000
        ),
    )(hist, idx)


def edge_kernel(vel_hbm, his_hbm, up_ref, down_ref, v_buf, h_buf, sems):
    copies = []
    for k, first in enumerate((NYL - 8, 0)):
        rows = pl.ds(first, 8)
        copies.append(
            (
                pltpu.make_async_copy(vel_hbm.at[:, :, rows, :], v_buf.at[k], sems.at[k]),
                pltpu.make_async_copy(his_hbm.at[:, :, rows, :], h_buf.at[k], sems.at[2 + k]),
            )
        )
    for pair in copies:
        for copy in pair:
            copy.start()
    for k, (out, row, one) in enumerate(((up_ref, 6, 7), (down_ref, 0, 0))):
        for copy in copies[k]:
            copy.wait()
        for layer in range(NXL):
            for c in range(3):
                out[layer, 2 * c : 2 * c + 2, :] = v_buf[k, c, layer, row : row + 2, :]
            for f in range(2):
                out[layer, 6 + f : 7 + f, :] = h_buf[k, f, layer, one : one + 1, :]


def edges(vel, hist):
    shape = jax.ShapeDtypeStruct((NXL, 8, NZ), F32)
    return pl.pallas_call(
        edge_kernel,
        in_specs=[pl.BlockSpec(memory_space=pl.ANY)] * 2,
        out_specs=in_vmem(2),
        out_shape=[shape, shape],
        scratch_shapes=[
            pltpu.VMEM((2, 3, NXL, 8, NZ), F32),
            pltpu.VMEM((2, 2, NXL, 8, NZ), F32),
            pltpu.SemaphoreType.DMA((4,)),
        ],
        compiler_params=pltpu.CompilerParams(vmem_limit_bytes=64 * MIB - EDGE_ROOM),
        name="edge_rows",
        cost_estimate=pl.CostEstimate(flops=100_000, transcendentals=0, bytes_accessed=1_000_000),
    )(vel, hist)


def span_keeps():
    b = lax.axis_index("span")
    keep_above = jnp.where(b == lax.axis_size("span") - 1, 0.0, 1.0)
    return jnp.where(b == 0, 0.0, 1.0), keep_above


def face_kernel(vel_ref, his_ref, below_ref, above_ref, right_ref, left_ref):
    a = lax.axis_index("stream")
    last = lax.axis_size("stream") - 1
    keep_below, keep_above = span_keeps()
    for out_ref, first, hist_layer, keep in (
        (right_ref, NXL - 2, NXL - 1, jnp.where(a == last, 0.0, 1.0)),
        (left_ref, 0, 0, jnp.where(a == 0, 0.0, 1.0)),
    ):
        for k in range(8):
            if k < 6:
                c, layer = k // 2, first + k % 2
                plane = vel_ref[c, layer]
                rows = slice(c * 2, c * 2 + 2)
                up, down = above_ref[layer, rows, :], below_ref[layer, rows, :]
            else:
                layer = hist_layer
                plane = his_ref[k - 6, layer]
                up, down = above_ref[layer, k : k + 1, :], below_ref[layer, k : k + 1, :]
            out_ref[k * NYL : (k + 1) * NYL, :] = plane * keep
            base, n = FACE + 4 * k, up.shape[0]
            out_ref[base : base + n, :] = up * (keep * keep_above)
            out_ref[base + 4 - n : base + 4, :] = down * (keep * keep_below)
            if n == 1:
                out_ref[base + 1 : base + 3, :] = jnp.zeros((2, NZ), F32)


def faces(vel, hist, below, above):
    shape = jax.ShapeDtypeStruct((FACE + 32, NZ), F32)
    return pl.pallas_call(
        face_kernel,
        in_specs=in_vmem(4),
        out_specs=in_vmem(2),
        out_shape=[shape, shape],
        compiler_params=params(4),
        name="face_layers",
        cost_estimate=pl.CostEstimate(flops=FACE_COST, transcendentals=0, bytes_accessed=1_200_000),
    )(vel, hist, below, above)


def add(a, b):
    return tuple(p + q for p, q in zip(a, b))


def sub(a, b):
    return tuple(p - q for p, q in zip(a, b))


def mul(a, b):
    return tuple(p * q for p, q in zip(a, b))


def each(fn, *a):
    return tuple(fn(*p) for p in zip(*a))


def y_next(a):
    return tuple(pltpu.roll(p, EXT - 1, 0) for p in a)


def y_prev(a):
    return tuple(pltpu.roll(p, 1, 0) for p in a)


def own(a):
    return tuple(p[:NYL] for p in a)


def z_prev(a, first, fill):
    lo, hi = a
    rlo, rhi = pltpu.roll(lo, 1, 1), pltpu.roll(hi, 1, 1)
    m = first[: lo.shape[0]]
    return jnp.where(m, fill, rlo), jnp.where(m, rlo, rhi)


def z_next(a, last, fill):
    lo, hi = a
    rlo, rhi = pltpu.roll(lo, ROW - 1, 1), pltpu.roll(hi, ROW - 1, 1)
    m = last[: lo.shape[0]]
    return jnp.where(m, rhi, rlo), jnp.where(m, fill, rhi)


def placement(dest_ref, w_ref, table_ref):
    dest = dest_ref[...]
    place = jnp.where(dest >= ROWS, -1, (dest % 2) * (ROWS // 2) + dest // 2).astype(F32)
    for c in range(CAP):
        table_ref[c : c + 1, :] = place[c : c + 1]
    table_ref[8:, :] = jnp.zeros((PEERS, ROW), F32)
    table_ref[8:, 0:8] = jnp.transpose(jnp.concatenate([w_ref[...]] * 4, axis=0))


def stencil_kernel(
    vel_hbm, his_hbm, xl_hbm, xr_hbm, below_ref, above_ref, dest_hbm, w_hbm,
    new_ref, mag_ref, table_ref,
    v_ref, h_ref, s_ref, corner_ref, dest_ref, w_ref, sems,
):
    a_id = lax.axis_index("stream")
    b_id = lax.axis_index("span")
    a_last = lax.axis_size("stream") - 1
    b_last = lax.axis_size("span") - 1
    halves = (slice(0, ROW), slice(ROW, NZ))

    copies = [
        pltpu.make_async_copy(
            ref.at[pl.ds(FACE, 32), :], corner_ref.at[side], sems.at[side]
        )
        for side, ref in enumerate((xl_hbm, xr_hbm))
    ]
    copies.append(pltpu.make_async_copy(dest_hbm, dest_ref, sems.at[38]))
    copies.append(pltpu.make_async_copy(w_hbm, w_ref, sems.at[39]))
    for z, cols in enumerate(halves):
        lanes = pl.ds(z * ROW, ROW)
        copies.append(
            pltpu.make_async_copy(
                vel_hbm.at[:, :, :, lanes],
                v_ref.at[:, pl.ds(2, NXL), z, pl.ds(0, NYL), :],
                sems.at[2 + z],
            )
        )
        copies.append(
            pltpu.make_async_copy(
                his_hbm.at[:, :, :, lanes],
                h_ref.at[:, pl.ds(1, NXL), z, pl.ds(0, NYL), :],
                sems.at[4 + z],
            )
        )
        for side, ref in enumerate((xl_hbm, xr_hbm)):
            for k in range(8):
                rows = pl.ds(k * NYL, NYL)
                if k < 6:
                    to = v_ref.at[k // 2, side * 10 + k % 2, z, pl.ds(0, NYL), :]
                else:
                    to = h_ref.at[k - 6, side * 9, z, pl.ds(0, NYL), :]
                copies.append(
                    pltpu.make_async_copy(
                        ref.at[rows, lanes], to, sems.at[6 + (side * 2 + z) * 8 + k]
                    )
                )
    for copy in copies:
        copy.start()

    zero4 = jnp.zeros((4, ROW), F32)
    keep_below, keep_above = span_keeps()

    def fill(ref, c, layer, z, up, down):
        n = up.shape[0]
        ref[c, layer, z, NYL : NYL + n, :] = up
        ref[c, layer, z, NYL + n : NYL + n + 4, :] = zero4
        ref[c, layer, z, NYL + 4 : EXT - n, :] = zero4[: 4 - n]
        ref[c, layer, z, EXT - n :, :] = down

    for z, cols in enumerate(halves):
        for layer in range(NXL):
            for c in range(3):
                rows = slice(c * 2, c * 2 + 2)
                up = above_ref[layer, rows, cols] * keep_above
                down = below_ref[layer, rows, cols] * keep_below
                fill(v_ref, c, layer + 2, z, up, down)
            for f in range(2):
                rows = slice(6 + f, 7 + f)
                up = above_ref[layer, rows, cols] * keep_above
                down = below_ref[layer, rows, cols] * keep_below
                fill(h_ref, f, layer + 1, z, up, down)
    for copy in copies:
        copy.wait()
    placement(dest_ref, w_ref, table_ref)
    for z, cols in enumerate(halves):
        for side in range(2):
            for k in range(8):
                n = 2 if k < 6 else 1
                up = corner_ref[side, 4 * k : 4 * k + n, cols]
                down = corner_ref[side, 4 * k + 4 - n : 4 * k + 4, cols]
                if k < 6:
                    fill(v_ref, k // 2, side * 10 + k % 2, z, up, down)
                else:
                    fill(h_ref, k - 6, side * 9, z, up, down)

    lane = lax.broadcasted_iota(jnp.int32, (EXT, ROW), 1)
    first, last = lane == 0, lane == ROW - 1
    row = lax.broadcasted_iota(jnp.int32, (EXT, ROW), 0)
    inside = jnp.where((row == 32) & (b_id == b_last), 0.0, 1.0) * jnp.where(
        (row == 39) & (b_id == 0), 0.0, 1.0
    )

    def get(ref, c, layer):
        return ref[c, layer, 0], ref[c, layer, 1]

    def smooth(below, mid, above):
        t = add(add(below, mid), add(mid, above))
        t = add(t, y_next(t))
        t = own(add(t, y_prev(t)))
        return add(add(t, t), add(z_prev(t, first, 0.0), z_next(t, last, 0.0)))

    def strain_layer(i, _):
        u = [get(v_ref, c, i + 1) for c in range(3)]
        keep = jnp.where(((i == 0) & (a_id == 0)) | ((i == 9) & (a_id == a_last)), 0.0, 1.0)
        m = inside * keep
        gx = [sub(get(v_ref, c, i + 2), get(v_ref, c, i)) for c in range(3)]
        gy = [sub(y_next(p), y_prev(p)) for p in u]
        gz = [sub(z_next(p, last, 0.0), z_prev(p, first, 0.0)) for p in u]
        t = [
            add(gx[0], gx[0]),
            add(gy[1], gy[1]),
            add(gz[2], gz[2]),
            add(gy[0], gx[1]),
            add(gz[0], gx[2]),
            add(gz[1], gy[2]),
        ]
        t = [each(lambda p: p * m, p) for p in t]
        q = [mul(p, p) for p in t]
        diag = add(add(q[0], q[1]), q[2])
        off = add(add(q[3], q[4]), q[5])
        mag = each(lambda p, r: jnp.sqrt((p + 2.0 * r) * 0.125), diag, off)

        @pl.when((i >= 1) & (i <= 8))
        def _():
            for z, cols in enumerate(halves):
                mag_ref[i - 1, :, cols] = mag[z][:NYL]

        for c in range(6):
            w = mul(mag, t[c])
            uu = mul(u[PAIRS[c][0]], u[PAIRS[c][1]])
            for z in range(2):
                s_ref[c, i, z] = t[c][z]
                s_ref[6 + c, i, z] = w[z]
                s_ref[12 + c, i, z] = uu[z]
        return 0

    lax.fori_loop(0, 10, strain_layer, 0)

    def close_layer(x, _):
        def hat(ref, c, at):
            return smooth(get(ref, c, at), get(ref, c, at + 1), get(ref, c, at + 2))

        s = [hat(s_ref, c, x) for c in range(6)]
        q = [mul(p, p) for p in s]
        diag = add(add(q[0], q[1]), q[2])
        off = add(add(q[3], q[4]), q[5])
        smag4 = each(lambda p, r: jnp.sqrt((p + 2.0 * r) * 0.125) * (4.0 / 64.0), diag, off)
        uh = [each(lambda p: p * (1.0 / 64.0), hat(v_ref, c, x + 1)) for c in range(3)]
        lm = mm = None
        for c in range(6):
            ms = hat(s_ref, 6 + c, x)
            m = each(lambda p, r, g: (p - g * r) * (1.0 / 128.0), ms, s[c], smag4)
            uu = hat(s_ref, 12 + c, x)
            ll = each(
                lambda p, r, g: p * (1.0 / 64.0) - r * g, uu, uh[PAIRS[c][0]], uh[PAIRS[c][1]]
            )
            m2 = m if c < 3 else add(m, m)
            dl, dm = mul(ll, m2), mul(m, m2)
            lm = dl if lm is None else add(lm, dl)
            mm = dm if mm is None else add(mm, dm)

        speed = [each(lambda p: DT * p, get(v_ref, c, x + 2)) for c in range(3)]
        moved = []
        for f in range(2):
            g = get(h_ref, f, x + 1)
            lower, upper = get(h_ref, f, x), get(h_ref, f, x + 2)

            def carry(mid, low, up, sp):
                return each(
                    lambda p, lo, hi, v: p + jnp.abs(v) * (jnp.where(v > 0, lo, hi) - p),
                    mid, low, up, sp,
                )

            g = carry(g, lower, upper, speed[0])
            g = carry(own(g), own(y_prev(g)), own(y_next(g)), own(speed[1]))
            g = carry(g, z_prev(g, first, 0.0), z_next(g, last, 0.0), own(speed[2]))
            moved.append(g)
        k = DT / 1.5
        for z, cols in enumerate(halves):
            m0, m1 = moved[0][z], moved[1][z]
            r = lax.rsqrt(lax.rsqrt(lax.rsqrt(m0 * m1)))
            blend = k / (r + k)
            new_ref[0, x, :, cols] = jnp.maximum(m0 + blend * (lm[z] - m0), 0.0)
            new_ref[1, x, :, cols] = m1 + blend * (mm[z] - m1)
        return 0

    lax.fori_loop(0, NXL, close_layer, 0)


def stencil(vel, hist, xl, xr, below, above, dest, weight):
    return pl.pallas_call(
        stencil_kernel,
        in_specs=[pl.BlockSpec(memory_space=pl.ANY)] * 4 + in_vmem(2) + [pl.BlockSpec(memory_space=pl.ANY)] * 2,
        out_specs=in_vmem(3),
        out_shape=[
            jax.ShapeDtypeStruct((2, NXL, NYL, NZ), F32),
            jax.ShapeDtypeStruct((NXL, NYL, NZ), F32),
            jax.ShapeDtypeStruct((8 + PEERS, ROW), F32),
        ],
        scratch_shapes=[
            pltpu.VMEM((3, 12, 2, EXT, ROW), F32),
            pltpu.VMEM((2, 10, 2, EXT, ROW), F32),
            pltpu.VMEM((18, 10, 2, EXT, ROW), F32),
            pltpu.VMEM((2, 32, NZ), F32),
            pltpu.VMEM((CAP, PEERS), jnp.int32),
            pltpu.VMEM((CAP, PEERS), F32),
            pltpu.SemaphoreType.DMA((40,)),
        ],
        compiler_params=params(16),
        name="stencil",
        cost_estimate=pl.CostEstimate(
            flops=STENCIL_COST, transcendentals=500_000, bytes_accessed=20_000_000
        ),
    )(vel, hist, xl, xr, below, above, dest, weight)


def place_kernel(new_ref, mag_ref, table_ref, got_ref, out_hbm, eddy_hbm, out_ref, eddy_ref, sems):
    ones = jnp.ones((CAP * PEERS, ROW), BF16)
    place = jnp.concatenate([table_ref[0:1, :], table_ref[1:2, :]], axis=1)
    rows = lax.broadcasted_iota(jnp.int32, (ROWS // 2, CAP * PEERS), 0).astype(F32)
    blended = []
    for c in range(CAP):
        wc = table_ref[8:, c : c + 1]
        cols = []
        for f in range(2):
            r0, r1 = got_ref[:, f * 4 + c * 2, :], got_ref[:, f * 4 + c * 2 + 1, :]
            cols.append(wc * r0 + (1.0 - wc) * r1)
        blended.append(jnp.concatenate(cols, axis=1))
    parts = split3(jnp.concatenate(blended, axis=0))
    copies = []
    for h in range(2):
        onehot = jnp.where(rows + float(h * ROWS // 2) == place, 1.0, 0.0).astype(BF16)
        acc = None
        for part in parts:
            d = jnp.dot(onehot, part, preferred_element_type=F32)
            acc = d if acc is None else acc + d
        hit = jnp.dot(onehot, ones, preferred_element_type=F32) > 0.5
        cols = slice(h * ROW, (h + 1) * ROW)
        lanes = pl.ds(h * ROW, ROW)
        final = []
        for f in range(2):
            cur = new_ref[f, :, :, cols].reshape(NXL * NYL, ROW)
            val = jnp.where(hit, acc[:, f * ROW : (f + 1) * ROW], cur)
            out_ref[h, f] = val.reshape(NXL, NYL, ROW)
            final.append(val)
        copy = pltpu.make_async_copy(out_ref.at[h], out_hbm.at[:, :, :, lanes], sems.at[h])
        copy.start()
        copies.append(copy)
        eddy = final[0] / final[1] * mag_ref[:, :, cols].reshape(NXL * NYL, ROW)
        eddy_ref[h] = eddy.reshape(NXL, NYL, ROW)
        copy = pltpu.make_async_copy(eddy_ref.at[h], eddy_hbm.at[:, :, lanes], sems.at[2 + h])
        copy.start()
        copies.append(copy)
    for copy in copies:
        copy.wait()


def place_rows(new, mag, table, got):
    return pl.pallas_call(
        place_kernel,
        in_specs=in_vmem(4),
        out_specs=[pl.BlockSpec(memory_space=pl.ANY)] * 2,
        out_shape=[
            jax.ShapeDtypeStruct((2, NXL, NYL, NZ), F32),
            jax.ShapeDtypeStruct((NXL, NYL, NZ), F32),
        ],
        scratch_shapes=[
            pltpu.VMEM((2, 2, NXL, NYL, ROW), F32),
            pltpu.VMEM((2, NXL, NYL, ROW), F32),
            pltpu.SemaphoreType.DMA((4,)),
        ],
        compiler_params=params(12),
        name="place_receptors",
        cost_estimate=pl.CostEstimate(
            flops=300_000_000, transcendentals=100_000, bytes_accessed=2_500_000
        ),
    )(new, mag, table, got)


def body(velocity, history, donor_rows, recv_dest, recv_weight):
    vel, hist = velocity[:, 0], history[:, 0]
    idx = jnp.transpose(donor_rows[0, 0, 0], (1, 2, 0)).reshape(2 * CAP, PEERS)

    up, down = edges(vel, hist)
    below = shift_ring(up, "span", 1)
    above = shift_ring(down, "span", -1)

    chosen = gather(hist, idx)
    chosen = lax.ppermute(chosen, "grid", [(0, 1), (1, 0)])
    got = lax.all_to_all(chosen, ("stream", "span"), split_axis=0, concat_axis=0, tiled=True)

    right, left = faces(vel, hist, below, above)
    xl = shift_ring(right, "stream", 1)
    xr = shift_ring(left, "stream", -1)
    dest = jnp.transpose(recv_dest[0, 0, 0])
    weight = jnp.transpose(recv_weight[0, 0, 0])
    made = stencil(vel, hist, xl, xr, below, above, dest, weight)
    final, eddy = place_rows(*made, got)
    return final[:, None], eddy[None]


def solution(mesh):
    in_specs = (
        P(None, "grid", "stream", "span", None),
        P(None, "grid", "stream", "span", None),
        P("grid", "stream", "span", None, None, None),
        P("grid", "stream", "span", None, None),
        P("grid", "stream", "span", None, None),
    )
    out_specs = (P(None, "grid", "stream", "span", None), P("grid", "stream", "span", None))
    return jax.shard_map(body, mesh=mesh, in_specs=in_specs, out_specs=out_specs, check_vma=False)
```

```python
import jax
import jax.numpy as jnp
from jax import lax
from jax.experimental import pallas as pl
from jax.experimental.pallas import tpu as pltpu
from jax.sharding import PartitionSpec as P

F32 = jnp.float32
BF16 = jnp.bfloat16
NXL, NYL, NZ, ROW = 8, 32, 256, 128
ROWS = 512
PEERS = 128
CAP = 2
FACE = 8 * NYL
EDGE_ROOM = 10500 * 1024
FACE_COST = 10_000_000_000
STENCIL_COST = 10_000_000_000
EXT = 40
DT = 0.2
MIB = 1024 * 1024
PAIRS = ((0, 0), (1, 1), (2, 2), (0, 1), (0, 2), (1, 2))


def in_vmem(n):
    return [pl.BlockSpec(memory_space=pltpu.VMEM)] * n


def params(mib):
    return pltpu.CompilerParams(vmem_limit_bytes=mib * MIB)


def shift_ring(x, axis, step):
    n = lax.axis_size(axis)
    return lax.ppermute(x, axis, [(i, (i + step) % n) for i in range(n)])


def split3(x):
    hi = x.astype(BF16)
    rest = x - hi.astype(F32)
    mid = rest.astype(BF16)
    low = (rest - mid.astype(F32)).astype(BF16)
    return hi, mid, low


def exact_dot(onehot, x):
    hi, mid, low = split3(x)
    out = jnp.dot(onehot, hi, preferred_element_type=F32)
    out = out + jnp.dot(onehot, mid, preferred_element_type=F32)
    return out + jnp.dot(onehot, low, preferred_element_type=F32)


def gather_kernel(hist_ref, idx_hbm, out_ref, idx_ref, sem):
    copy = pltpu.make_async_copy(idx_hbm, idx_ref, sem)
    copy.start()
    halves = []
    for h in range(2):
        cols = [
            hist_ref[f, :, :, h * ROW : (h + 1) * ROW].reshape(NXL * NYL, ROW)
            for f in range(2)
        ]
        halves.append(split3(jnp.concatenate(cols, axis=1)))
    copy.wait()
    idx = idx_ref[...]
    place = (idx % 2) * (ROWS // 2) + idx // 2
    place = jnp.transpose(jnp.concatenate([place, place], axis=0).astype(F32))
    lanes = lax.broadcasted_iota(jnp.int32, (PEERS, ROWS // 2), 1).astype(F32)
    for j in range(2 * CAP):
        col = place[:, j : j + 1]
        acc = None
        for h in range(2):
            onehot = jnp.where(lanes + float(h * ROWS // 2) == col, 1.0, 0.0).astype(BF16)
            for part in halves[h]:
                d = jnp.dot(onehot, part, preferred_element_type=F32)
                acc = d if acc is None else acc + d
        for f in range(2):
            out_ref[:, f * 4 + j, :] = acc[:, f * ROW : (f + 1) * ROW]


def gather(hist, idx):
    return pl.pallas_call(
        gather_kernel,
        in_specs=in_vmem(1) + [pl.BlockSpec(memory_space=pl.ANY)],
        out_specs=in_vmem(1)[0],
        scratch_shapes=[
            pltpu.VMEM((2 * CAP, PEERS), jnp.int32),
            pltpu.SemaphoreType.DMA(()),
        ],
        out_shape=jax.ShapeDtypeStruct((PEERS, 8, ROW), F32),
        compiler_params=params(8),
        name="pick_donors",
        cost_estimate=pl.CostEstimate(
            flops=400_000_000, transcendentals=0, bytes_accessed=1_100_000
        ),
    )(hist, idx)


def edge_kernel(vel_hbm, his_hbm, up_ref, down_ref, sems):
    copies = []
    for side, (out, v_row, h_row) in enumerate(
        ((up_ref, NYL - 2, NYL - 1), (down_ref, 0, 0))
    ):
        for c in range(3):
            copies.append(
                pltpu.make_async_copy(
                    vel_hbm.at[c, :, pl.ds(v_row, 2), :],
                    out.at[:, pl.ds(2 * c, 2), :],
                    sems.at[side, c],
                )
            )
        for f in range(2):
            copies.append(
                pltpu.make_async_copy(
                    his_hbm.at[f, :, pl.ds(h_row, 1), :],
                    out.at[:, pl.ds(6 + f, 1), :],
                    sems.at[side, 3 + f],
                )
            )
    for copy in copies:
        copy.start()
    for copy in copies:
        copy.wait()


def edges(vel, hist):
    shape = jax.ShapeDtypeStruct((NXL, 8, NZ), F32)
    return pl.pallas_call(
        edge_kernel,
        in_specs=[pl.BlockSpec(memory_space=pl.ANY)] * 2,
        out_specs=in_vmem(2),
        out_shape=[shape, shape],
        scratch_shapes=[
            pltpu.SemaphoreType.DMA((2, 5)),
        ],
        compiler_params=pltpu.CompilerParams(vmem_limit_bytes=64 * MIB - EDGE_ROOM),
        name="edge_rows",
        cost_estimate=pl.CostEstimate(flops=100_000, transcendentals=0, bytes_accessed=1_000_000),
    )(vel, hist)


def span_keeps():
    b = lax.axis_index("span")
    keep_above = jnp.where(b == lax.axis_size("span") - 1, 0.0, 1.0)
    return jnp.where(b == 0, 0.0, 1.0), keep_above


def face_kernel(vel_ref, his_ref, below_ref, above_ref, right_ref, left_ref):
    a = lax.axis_index("stream")
    last = lax.axis_size("stream") - 1
    keep_below, keep_above = span_keeps()
    for out_ref, first, hist_layer, keep in (
        (right_ref, NXL - 2, NXL - 1, jnp.where(a == last, 0.0, 1.0)),
        (left_ref, 0, 0, jnp.where(a == 0, 0.0, 1.0)),
    ):
        for k in range(8):
            if k < 6:
                c, layer = k // 2, first + k % 2
                plane = vel_ref[c, layer]
                rows = slice(c * 2, c * 2 + 2)
                up, down = above_ref[layer, rows, :], below_ref[layer, rows, :]
            else:
                layer = hist_layer
                plane = his_ref[k - 6, layer]
                up, down = above_ref[layer, k : k + 1, :], below_ref[layer, k : k + 1, :]
            out_ref[k * NYL : (k + 1) * NYL, :] = plane * keep
            base, n = FACE + 4 * k, up.shape[0]
            out_ref[base : base + n, :] = up * (keep * keep_above)
            out_ref[base + 4 - n : base + 4, :] = down * (keep * keep_below)
            if n == 1:
                out_ref[base + 1 : base + 3, :] = jnp.zeros((2, NZ), F32)


def faces(vel, hist, below, above):
    shape = jax.ShapeDtypeStruct((FACE + 32, NZ), F32)
    return pl.pallas_call(
        face_kernel,
        in_specs=in_vmem(4),
        out_specs=in_vmem(2),
        out_shape=[shape, shape],
        compiler_params=params(4),
        name="face_layers",
        cost_estimate=pl.CostEstimate(flops=FACE_COST, transcendentals=0, bytes_accessed=1_200_000),
    )(vel, hist, below, above)


def add(a, b):
    return tuple(p + q for p, q in zip(a, b))


def sub(a, b):
    return tuple(p - q for p, q in zip(a, b))


def mul(a, b):
    return tuple(p * q for p, q in zip(a, b))


def each(fn, *a):
    return tuple(fn(*p) for p in zip(*a))


def y_next(a):
    return tuple(pltpu.roll(p, EXT - 1, 0) for p in a)


def y_prev(a):
    return tuple(pltpu.roll(p, 1, 0) for p in a)


def own(a):
    return tuple(p[:NYL] for p in a)


def z_prev(a, first, fill):
    lo, hi = a
    rlo, rhi = pltpu.roll(lo, 1, 1), pltpu.roll(hi, 1, 1)
    m = first[: lo.shape[0]]
    return jnp.where(m, fill, rlo), jnp.where(m, rlo, rhi)


def z_next(a, last, fill):
    lo, hi = a
    rlo, rhi = pltpu.roll(lo, ROW - 1, 1), pltpu.roll(hi, ROW - 1, 1)
    m = last[: lo.shape[0]]
    return jnp.where(m, rhi, rlo), jnp.where(m, fill, rhi)


def placement(dest_ref, w_ref, table_ref):
    dest = dest_ref[...]
    place = jnp.where(dest >= ROWS, -1, (dest % 2) * (ROWS // 2) + dest // 2).astype(F32)
    for c in range(CAP):
        table_ref[c : c + 1, :] = place[c : c + 1]
    table_ref[8:, :] = jnp.zeros((PEERS, ROW), F32)
    table_ref[8:, 0:8] = jnp.transpose(jnp.concatenate([w_ref[...]] * 4, axis=0))


def stencil_kernel(
    vel_hbm, his_hbm, xl_hbm, xr_hbm, below_ref, above_ref, dest_hbm, w_hbm,
    new_ref, mag_ref, table_ref,
    v_ref, h_ref, s_ref, corner_ref, dest_ref, w_ref, sems,
):
    a_id = lax.axis_index("stream")
    b_id = lax.axis_index("span")
    a_last = lax.axis_size("stream") - 1
    b_last = lax.axis_size("span") - 1
    halves = (slice(0, ROW), slice(ROW, NZ))

    copies = [
        pltpu.make_async_copy(
            ref.at[pl.ds(FACE, 32), :], corner_ref.at[side], sems.at[side]
        )
        for side, ref in enumerate((xl_hbm, xr_hbm))
    ]
    copies.append(pltpu.make_async_copy(dest_hbm, dest_ref, sems.at[38]))
    copies.append(pltpu.make_async_copy(w_hbm, w_ref, sems.at[39]))
    for z, cols in enumerate(halves):
        lanes = pl.ds(z * ROW, ROW)
        copies.append(
            pltpu.make_async_copy(
                vel_hbm.at[:, :, :, lanes],
                v_ref.at[:, pl.ds(2, NXL), z, pl.ds(0, NYL), :],
                sems.at[2 + z],
            )
        )
        copies.append(
            pltpu.make_async_copy(
                his_hbm.at[:, :, :, lanes],
                h_ref.at[:, pl.ds(1, NXL), z, pl.ds(0, NYL), :],
                sems.at[4 + z],
            )
        )
        for side, ref in enumerate((xl_hbm, xr_hbm)):
            for k in range(8):
                rows = pl.ds(k * NYL, NYL)
                if k < 6:
                    to = v_ref.at[k // 2, side * 10 + k % 2, z, pl.ds(0, NYL), :]
                else:
                    to = h_ref.at[k - 6, side * 9, z, pl.ds(0, NYL), :]
                copies.append(
                    pltpu.make_async_copy(
                        ref.at[rows, lanes], to, sems.at[6 + (side * 2 + z) * 8 + k]
                    )
                )
    for copy in copies:
        copy.start()

    zero4 = jnp.zeros((4, ROW), F32)
    keep_below, keep_above = span_keeps()

    def fill(ref, c, layer, z, up, down):
        n = up.shape[0]
        ref[c, layer, z, NYL : NYL + n, :] = up
        ref[c, layer, z, NYL + n : NYL + n + 4, :] = zero4
        ref[c, layer, z, NYL + 4 : EXT - n, :] = zero4[: 4 - n]
        ref[c, layer, z, EXT - n :, :] = down

    for z, cols in enumerate(halves):
        for layer in range(NXL):
            for c in range(3):
                rows = slice(c * 2, c * 2 + 2)
                up = above_ref[layer, rows, cols] * keep_above
                down = below_ref[layer, rows, cols] * keep_below
                fill(v_ref, c, layer + 2, z, up, down)
            for f in range(2):
                rows = slice(6 + f, 7 + f)
                up = above_ref[layer, rows, cols] * keep_above
                down = below_ref[layer, rows, cols] * keep_below
                fill(h_ref, f, layer + 1, z, up, down)
    for copy in copies:
        copy.wait()
    placement(dest_ref, w_ref, table_ref)
    for z, cols in enumerate(halves):
        for side in range(2):
            for k in range(8):
                n = 2 if k < 6 else 1
                up = corner_ref[side, 4 * k : 4 * k + n, cols]
                down = corner_ref[side, 4 * k + 4 - n : 4 * k + 4, cols]
                if k < 6:
                    fill(v_ref, k // 2, side * 10 + k % 2, z, up, down)
                else:
                    fill(h_ref, k - 6, side * 9, z, up, down)

    lane = lax.broadcasted_iota(jnp.int32, (EXT, ROW), 1)
    first, last = lane == 0, lane == ROW - 1
    row = lax.broadcasted_iota(jnp.int32, (EXT, ROW), 0)
    inside = jnp.where((row == 32) & (b_id == b_last), 0.0, 1.0) * jnp.where(
        (row == 39) & (b_id == 0), 0.0, 1.0
    )

    def get(ref, c, layer):
        return ref[c, layer, 0], ref[c, layer, 1]

    def smooth(below, mid, above):
        t = add(add(below, mid), add(mid, above))
        t = add(t, y_next(t))
        t = own(add(t, y_prev(t)))
        return add(add(t, t), add(z_prev(t, first, 0.0), z_next(t, last, 0.0)))

    def strain_layer(i, _):
        u = [get(v_ref, c, i + 1) for c in range(3)]
        keep = jnp.where(((i == 0) & (a_id == 0)) | ((i == 9) & (a_id == a_last)), 0.0, 1.0)
        m = inside * keep
        gx = [sub(get(v_ref, c, i + 2), get(v_ref, c, i)) for c in range(3)]
        gy = [sub(y_next(p), y_prev(p)) for p in u]
        gz = [sub(z_next(p, last, 0.0), z_prev(p, first, 0.0)) for p in u]
        t = [
            add(gx[0], gx[0]),
            add(gy[1], gy[1]),
            add(gz[2], gz[2]),
            add(gy[0], gx[1]),
            add(gz[0], gx[2]),
            add(gz[1], gy[2]),
        ]
        t = [each(lambda p: p * m, p) for p in t]
        q = [mul(p, p) for p in t]
        diag = add(add(q[0], q[1]), q[2])
        off = add(add(q[3], q[4]), q[5])
        mag = each(lambda p, r: jnp.sqrt((p + 2.0 * r) * 0.125), diag, off)

        @pl.when((i >= 1) & (i <= 8))
        def _():
            for z, cols in enumerate(halves):
                mag_ref[i - 1, :, cols] = mag[z][:NYL]

        for c in range(6):
            w = mul(mag, t[c])
            uu = mul(u[PAIRS[c][0]], u[PAIRS[c][1]])
            for z in range(2):
                s_ref[c, i, z] = t[c][z]
                s_ref[6 + c, i, z] = w[z]
                s_ref[12 + c, i, z] = uu[z]
        return 0

    lax.fori_loop(0, 10, strain_layer, 0)

    def close_layer(x, _):
        def hat(ref, c, at):
            return smooth(get(ref, c, at), get(ref, c, at + 1), get(ref, c, at + 2))

        s = [hat(s_ref, c, x) for c in range(6)]
        q = [mul(p, p) for p in s]
        diag = add(add(q[0], q[1]), q[2])
        off = add(add(q[3], q[4]), q[5])
        smag4 = each(lambda p, r: jnp.sqrt((p + 2.0 * r) * 0.125) * (4.0 / 64.0), diag, off)
        uh = [each(lambda p: p * (1.0 / 64.0), hat(v_ref, c, x + 1)) for c in range(3)]
        lm = mm = None
        for c in range(6):
            ms = hat(s_ref, 6 + c, x)
            m = each(lambda p, r, g: (p - g * r) * (1.0 / 128.0), ms, s[c], smag4)
            uu = hat(s_ref, 12 + c, x)
            ll = each(
                lambda p, r, g: p * (1.0 / 64.0) - r * g, uu, uh[PAIRS[c][0]], uh[PAIRS[c][1]]
            )
            m2 = m if c < 3 else add(m, m)
            dl, dm = mul(ll, m2), mul(m, m2)
            lm = dl if lm is None else add(lm, dl)
            mm = dm if mm is None else add(mm, dm)

        speed = [each(lambda p: DT * p, get(v_ref, c, x + 2)) for c in range(3)]
        moved = []
        for f in range(2):
            g = get(h_ref, f, x + 1)
            lower, upper = get(h_ref, f, x), get(h_ref, f, x + 2)

            def carry(mid, low, up, sp):
                return each(
                    lambda p, lo, hi, v: p + jnp.abs(v) * (jnp.where(v > 0, lo, hi) - p),
                    mid, low, up, sp,
                )

            g = carry(g, lower, upper, speed[0])
            g = carry(own(g), own(y_prev(g)), own(y_next(g)), own(speed[1]))
            g = carry(g, z_prev(g, first, 0.0), z_next(g, last, 0.0), own(speed[2]))
            moved.append(g)
        k = DT / 1.5
        for z, cols in enumerate(halves):
            m0, m1 = moved[0][z], moved[1][z]
            r = lax.rsqrt(lax.rsqrt(lax.rsqrt(m0 * m1)))
            blend = k / (r + k)
            new_ref[0, x, :, cols] = jnp.maximum(m0 + blend * (lm[z] - m0), 0.0)
            new_ref[1, x, :, cols] = m1 + blend * (mm[z] - m1)
        return 0

    lax.fori_loop(0, NXL, close_layer, 0)


def stencil(vel, hist, xl, xr, below, above, dest, weight):
    return pl.pallas_call(
        stencil_kernel,
        in_specs=[pl.BlockSpec(memory_space=pl.ANY)] * 4 + in_vmem(2) + [pl.BlockSpec(memory_space=pl.ANY)] * 2,
        out_specs=in_vmem(3),
        out_shape=[
            jax.ShapeDtypeStruct((2, NXL, NYL, NZ), F32),
            jax.ShapeDtypeStruct((NXL, NYL, NZ), F32),
            jax.ShapeDtypeStruct((8 + PEERS, ROW), F32),
        ],
        scratch_shapes=[
            pltpu.VMEM((3, 12, 2, EXT, ROW), F32),
            pltpu.VMEM((2, 10, 2, EXT, ROW), F32),
            pltpu.VMEM((18, 10, 2, EXT, ROW), F32),
            pltpu.VMEM((2, 32, NZ), F32),
            pltpu.VMEM((CAP, PEERS), jnp.int32),
            pltpu.VMEM((CAP, PEERS), F32),
            pltpu.SemaphoreType.DMA((40,)),
        ],
        compiler_params=params(16),
        name="stencil",
        cost_estimate=pl.CostEstimate(
            flops=STENCIL_COST, transcendentals=500_000, bytes_accessed=20_000_000
        ),
    )(vel, hist, xl, xr, below, above, dest, weight)


def place_kernel(new_ref, mag_ref, table_ref, got_ref, out_hbm, eddy_hbm, out_ref, eddy_ref, sems):
    half = NXL // 2
    n = half * NYL
    ones = jnp.ones((CAP * PEERS, ROW), BF16)
    place = jnp.concatenate([table_ref[0:1, :], table_ref[1:2, :]], axis=1)
    rows = lax.broadcasted_iota(jnp.int32, (n, CAP * PEERS), 0).astype(F32)
    blended = []
    for c in range(CAP):
        wc = table_ref[8:, c : c + 1]
        cols = []
        for f in range(2):
            r0, r1 = got_ref[:, f * 4 + c * 2, :], got_ref[:, f * 4 + c * 2 + 1, :]
            cols.append(wc * r0 + (1.0 - wc) * r1)
        blended.append(jnp.concatenate(cols, axis=1))
    parts = split3(jnp.concatenate(blended, axis=0))
    copies = []
    for stage in range(4):
        h, q = stage // 2, stage % 2
        onehot = jnp.where(rows + float(stage * n) == place, 1.0, 0.0).astype(BF16)
        acc = None
        for part in parts:
            d = jnp.dot(onehot, part, preferred_element_type=F32)
            acc = d if acc is None else acc + d
        hit = jnp.dot(onehot, ones, preferred_element_type=F32) > 0.5
        cols = slice(h * ROW, (h + 1) * ROW)
        layers = slice(q * half, (q + 1) * half)
        at, lanes = pl.ds(q * half, half), pl.ds(h * ROW, ROW)
        final = []
        for f in range(2):
            cur = new_ref[f, layers, :, cols].reshape(n, ROW)
            val = jnp.where(hit, acc[:, f * ROW : (f + 1) * ROW], cur)
            out_ref[stage, f] = val.reshape(half, NYL, ROW)
            final.append(val)
        copies.append(
            pltpu.make_async_copy(out_ref.at[stage], out_hbm.at[:, at, :, lanes], sems.at[0, stage])
        )
        copies[-1].start()
        eddy = final[0] / final[1] * mag_ref[layers, :, cols].reshape(n, ROW)
        eddy_ref[stage] = eddy.reshape(half, NYL, ROW)
        copies.append(
            pltpu.make_async_copy(eddy_ref.at[stage], eddy_hbm.at[at, :, lanes], sems.at[1, stage])
        )
        copies[-1].start()
    for copy in copies:
        copy.wait()


def place_rows(new, mag, table, got):
    return pl.pallas_call(
        place_kernel,
        in_specs=in_vmem(4),
        out_specs=[pl.BlockSpec(memory_space=pl.ANY)] * 2,
        out_shape=[
            jax.ShapeDtypeStruct((2, NXL, NYL, NZ), F32),
            jax.ShapeDtypeStruct((NXL, NYL, NZ), F32),
        ],
        scratch_shapes=[
            pltpu.VMEM((4, 2, NXL // 2, NYL, ROW), F32),
            pltpu.VMEM((4, NXL // 2, NYL, ROW), F32),
            pltpu.SemaphoreType.DMA((2, 4)),
        ],
        compiler_params=params(12),
        name="place_receptors",
        cost_estimate=pl.CostEstimate(
            flops=300_000_000, transcendentals=100_000, bytes_accessed=2_500_000
        ),
    )(new, mag, table, got)


def body(velocity, history, donor_rows, recv_dest, recv_weight):
    vel, hist = velocity[:, 0], history[:, 0]
    idx = jnp.transpose(donor_rows[0, 0, 0], (1, 2, 0)).reshape(2 * CAP, PEERS)

    up, down = edges(vel, hist)
    below = shift_ring(up, "span", 1)
    above = shift_ring(down, "span", -1)

    chosen = gather(hist, idx)
    chosen = lax.ppermute(chosen, "grid", [(0, 1), (1, 0)])
    chosen = chosen.reshape(PEERS, 1, 8 * ROW)
    got = lax.all_to_all(chosen, ("stream", "span"), split_axis=0, concat_axis=0, tiled=True)
    got = got.reshape(PEERS, 8, ROW)

    right, left = faces(vel, hist, below, above)
    xl = shift_ring(right, "stream", 1)
    xr = shift_ring(left, "stream", -1)
    dest = jnp.transpose(recv_dest[0, 0, 0])
    weight = jnp.transpose(recv_weight[0, 0, 0])
    made = stencil(vel, hist, xl, xr, below, above, dest, weight)
    final, eddy = place_rows(*made, got)
    return final[:, None], eddy[None]


def solution(mesh):
    in_specs = (
        P(None, "grid", "stream", "span", None),
        P(None, "grid", "stream", "span", None),
        P("grid", "stream", "span", None, None, None),
        P("grid", "stream", "span", None, None),
        P("grid", "stream", "span", None, None),
    )
    out_specs = (P(None, "grid", "stream", "span", None), P("grid", "stream", "span", None))
    return jax.shard_map(body, mesh=mesh, in_specs=in_specs, out_specs=out_specs, check_vma=False)
```

```python
import jax
import jax.numpy as jnp
from jax import lax
from jax.experimental import pallas as pl
from jax.experimental.pallas import tpu as pltpu
from jax.sharding import PartitionSpec as P

F32 = jnp.float32
BF16 = jnp.bfloat16
NXL, NYL, NZ, ROW = 8, 32, 256, 128
ROWS = 512
PEERS = 128
CAP = 2
FACE = 8 * NYL
EDGE_ROOM = 10500 * 1024
FACE_COST = 10_000_000_000
STENCIL_COST = 10_000_000_000
EXT = 40
DT = 0.2
MIB = 1024 * 1024
PAIRS = ((0, 0), (1, 1), (2, 2), (0, 1), (0, 2), (1, 2))


def in_vmem(n):
    return [pl.BlockSpec(memory_space=pltpu.VMEM)] * n


def params(mib):
    return pltpu.CompilerParams(vmem_limit_bytes=mib * MIB)


def shift_ring(x, axis, step):
    n = lax.axis_size(axis)
    return lax.ppermute(x, axis, [(i, (i + step) % n) for i in range(n)])


def split3(x):
    hi = x.astype(BF16)
    rest = x - hi.astype(F32)
    mid = rest.astype(BF16)
    low = (rest - mid.astype(F32)).astype(BF16)
    return hi, mid, low


def gather_kernel(hist_ref, idx_hbm, out_ref, idx_ref, sem):
    copy = pltpu.make_async_copy(idx_hbm, idx_ref, sem)
    copy.start()
    halves = []
    for h in range(2):
        cols = [
            hist_ref[f, :, :, h * ROW : (h + 1) * ROW].reshape(NXL * NYL, ROW)
            for f in range(2)
        ]
        halves.append(split3(jnp.concatenate(cols, axis=1)))
    copy.wait()
    idx = idx_ref[...]
    place = (idx % 2) * (ROWS // 2) + idx // 2
    place = jnp.transpose(jnp.concatenate([place, place], axis=0).astype(F32))
    lanes = lax.broadcasted_iota(jnp.int32, (PEERS, ROWS // 2), 1).astype(F32)
    for j in range(2 * CAP):
        col = place[:, j : j + 1]
        acc = None
        for h in range(2):
            onehot = jnp.where(lanes + float(h * ROWS // 2) == col, 1.0, 0.0).astype(BF16)
            for part in halves[h]:
                d = jnp.dot(onehot, part, preferred_element_type=F32)
                acc = d if acc is None else acc + d
        for f in range(2):
            out_ref[:, f * 4 + j, :] = acc[:, f * ROW : (f + 1) * ROW]


def gather(hist, idx):
    return pl.pallas_call(
        gather_kernel,
        in_specs=in_vmem(1) + [pl.BlockSpec(memory_space=pl.ANY)],
        out_specs=in_vmem(1)[0],
        scratch_shapes=[
            pltpu.VMEM((2 * CAP, PEERS), jnp.int32),
            pltpu.SemaphoreType.DMA(()),
        ],
        out_shape=jax.ShapeDtypeStruct((PEERS, 8, ROW), F32),
        compiler_params=params(8),
        name="pick_donors",
        cost_estimate=pl.CostEstimate(
            flops=400_000_000, transcendentals=0, bytes_accessed=1_100_000
        ),
    )(hist, idx)


def edge_kernel(vel_hbm, his_hbm, up_ref, down_ref, sems):
    copies = []
    for side, (out, v_row, h_row) in enumerate(
        ((up_ref, NYL - 2, NYL - 1), (down_ref, 0, 0))
    ):
        for c in range(3):
            copies.append(
                pltpu.make_async_copy(
                    vel_hbm.at[c, :, pl.ds(v_row, 2), :],
                    out.at[:, pl.ds(2 * c, 2), :],
                    sems.at[side, c],
                )
            )
        for f in range(2):
            copies.append(
                pltpu.make_async_copy(
                    his_hbm.at[f, :, pl.ds(h_row, 1), :],
                    out.at[:, pl.ds(6 + f, 1), :],
                    sems.at[side, 3 + f],
                )
            )
    for copy in copies:
        copy.start()
    for copy in copies:
        copy.wait()


def edges(vel, hist):
    shape = jax.ShapeDtypeStruct((NXL, 8, NZ), F32)
    return pl.pallas_call(
        edge_kernel,
        in_specs=[pl.BlockSpec(memory_space=pl.ANY)] * 2,
        out_specs=in_vmem(2),
        out_shape=[shape, shape],
        scratch_shapes=[
            pltpu.SemaphoreType.DMA((2, 5)),
        ],
        compiler_params=pltpu.CompilerParams(vmem_limit_bytes=64 * MIB - EDGE_ROOM),
        name="edge_rows",
        cost_estimate=pl.CostEstimate(flops=100_000, transcendentals=0, bytes_accessed=1_000_000),
    )(vel, hist)


def span_keeps():
    b = lax.axis_index("span")
    keep_above = jnp.where(b == lax.axis_size("span") - 1, 0.0, 1.0)
    return jnp.where(b == 0, 0.0, 1.0), keep_above


def face_kernel(vel_ref, his_ref, below_ref, above_ref, right_ref, left_ref):
    a = lax.axis_index("stream")
    last = lax.axis_size("stream") - 1
    keep_below, keep_above = span_keeps()
    for out_ref, first, hist_layer, keep in (
        (right_ref, NXL - 2, NXL - 1, jnp.where(a == last, 0.0, 1.0)),
        (left_ref, 0, 0, jnp.where(a == 0, 0.0, 1.0)),
    ):
        for k in range(8):
            if k < 6:
                c, layer = k // 2, first + k % 2
                plane = vel_ref[c, layer]
                rows = slice(c * 2, c * 2 + 2)
                up, down = above_ref[layer, rows, :], below_ref[layer, rows, :]
            else:
                layer = hist_layer
                plane = his_ref[k - 6, layer]
                up, down = above_ref[layer, k : k + 1, :], below_ref[layer, k : k + 1, :]
            out_ref[k * NYL : (k + 1) * NYL, :] = plane * keep
            base, n = FACE + 4 * k, up.shape[0]
            out_ref[base : base + n, :] = up * (keep * keep_above)
            out_ref[base + 4 - n : base + 4, :] = down * (keep * keep_below)
            if n == 1:
                out_ref[base + 1 : base + 3, :] = jnp.zeros((2, NZ), F32)


def faces(vel, hist, below, above):
    shape = jax.ShapeDtypeStruct((FACE + 32, NZ), F32)
    return pl.pallas_call(
        face_kernel,
        in_specs=in_vmem(4),
        out_specs=in_vmem(2),
        out_shape=[shape, shape],
        compiler_params=params(4),
        name="face_layers",
        cost_estimate=pl.CostEstimate(flops=FACE_COST, transcendentals=0, bytes_accessed=1_200_000),
    )(vel, hist, below, above)


def add(a, b):
    return tuple(p + q for p, q in zip(a, b))


def sub(a, b):
    return tuple(p - q for p, q in zip(a, b))


def mul(a, b):
    return tuple(p * q for p, q in zip(a, b))


def each(fn, *a):
    return tuple(fn(*p) for p in zip(*a))


def y_next(a):
    return tuple(pltpu.roll(p, EXT - 1, 0) for p in a)


def y_prev(a):
    return tuple(pltpu.roll(p, 1, 0) for p in a)


def own(a):
    return tuple(p[:NYL] for p in a)


def z_prev(a, first, fill):
    lo, hi = a
    rlo, rhi = pltpu.roll(lo, 1, 1), pltpu.roll(hi, 1, 1)
    m = first[: lo.shape[0]]
    return jnp.where(m, fill, rlo), jnp.where(m, rlo, rhi)


def z_next(a, last, fill):
    lo, hi = a
    rlo, rhi = pltpu.roll(lo, ROW - 1, 1), pltpu.roll(hi, ROW - 1, 1)
    m = last[: lo.shape[0]]
    return jnp.where(m, rhi, rlo), jnp.where(m, fill, rhi)


def placement(dest_ref, w_ref, table_ref, hit_ref):
    dest = dest_ref[...]
    place = jnp.where(dest >= ROWS, -1, (dest % 2) * (ROWS // 2) + dest // 2).astype(F32)
    for c in range(CAP):
        table_ref[c : c + 1, :] = place[c : c + 1]
    table_ref[8:, :] = jnp.zeros((PEERS, ROW), F32)
    table_ref[8:, 0:8] = jnp.transpose(jnp.concatenate([w_ref[...]] * 4, axis=0))
    ones = jnp.ones((CAP * PEERS, ROW), BF16)
    place = jnp.concatenate([place[0:1], place[1:2]], axis=1)
    rows = lax.broadcasted_iota(jnp.int32, (ROWS // 2, CAP * PEERS), 0).astype(F32)
    for h in range(2):
        onehot = jnp.where(rows + float(h * ROWS // 2) == place, 1.0, 0.0).astype(BF16)
        hit_ref[h] = jnp.dot(onehot, ones, preferred_element_type=F32)


def stencil_kernel(
    vel_hbm, his_hbm, xl_hbm, xr_hbm, below_ref, above_ref, dest_hbm, w_hbm,
    new_ref, mag_ref, table_ref,
    v_ref, h_ref, s_ref, corner_ref, hit_ref, dest_ref, w_ref, sems,
):
    a_id = lax.axis_index("stream")
    b_id = lax.axis_index("span")
    a_last = lax.axis_size("stream") - 1
    b_last = lax.axis_size("span") - 1
    halves = (slice(0, ROW), slice(ROW, NZ))

    copies = [
        pltpu.make_async_copy(
            ref.at[pl.ds(FACE, 32), :], corner_ref.at[side], sems.at[side]
        )
        for side, ref in enumerate((xl_hbm, xr_hbm))
    ]
    copies.append(pltpu.make_async_copy(dest_hbm, dest_ref, sems.at[38]))
    copies.append(pltpu.make_async_copy(w_hbm, w_ref, sems.at[39]))
    for z, cols in enumerate(halves):
        lanes = pl.ds(z * ROW, ROW)
        copies.append(
            pltpu.make_async_copy(
                vel_hbm.at[:, :, :, lanes],
                v_ref.at[:, pl.ds(2, NXL), z, pl.ds(0, NYL), :],
                sems.at[2 + z],
            )
        )
        copies.append(
            pltpu.make_async_copy(
                his_hbm.at[:, :, :, lanes],
                h_ref.at[:, pl.ds(1, NXL), z, pl.ds(0, NYL), :],
                sems.at[4 + z],
            )
        )
        for side, ref in enumerate((xl_hbm, xr_hbm)):
            for k in range(8):
                rows = pl.ds(k * NYL, NYL)
                if k < 6:
                    to = v_ref.at[k // 2, side * 10 + k % 2, z, pl.ds(0, NYL), :]
                else:
                    to = h_ref.at[k - 6, side * 9, z, pl.ds(0, NYL), :]
                copies.append(
                    pltpu.make_async_copy(
                        ref.at[rows, lanes], to, sems.at[6 + (side * 2 + z) * 8 + k]
                    )
                )
    for copy in copies:
        copy.start()

    zero4 = jnp.zeros((4, ROW), F32)
    keep_below, keep_above = span_keeps()

    def fill(ref, c, layer, z, up, down):
        n = up.shape[0]
        ref[c, layer, z, NYL : NYL + n, :] = up
        ref[c, layer, z, NYL + n : NYL + n + 4, :] = zero4
        ref[c, layer, z, NYL + 4 : EXT - n, :] = zero4[: 4 - n]
        ref[c, layer, z, EXT - n :, :] = down

    for z, cols in enumerate(halves):
        for layer in range(NXL):
            for c in range(3):
                rows = slice(c * 2, c * 2 + 2)
                up = above_ref[layer, rows, cols] * keep_above
                down = below_ref[layer, rows, cols] * keep_below
                fill(v_ref, c, layer + 2, z, up, down)
            for f in range(2):
                rows = slice(6 + f, 7 + f)
                up = above_ref[layer, rows, cols] * keep_above
                down = below_ref[layer, rows, cols] * keep_below
                fill(h_ref, f, layer + 1, z, up, down)
    for copy in copies:
        copy.wait()
    placement(dest_ref, w_ref, table_ref, hit_ref)
    for z, cols in enumerate(halves):
        for side in range(2):
            for k in range(8):
                n = 2 if k < 6 else 1
                up = corner_ref[side, 4 * k : 4 * k + n, cols]
                down = corner_ref[side, 4 * k + 4 - n : 4 * k + 4, cols]
                if k < 6:
                    fill(v_ref, k // 2, side * 10 + k % 2, z, up, down)
                else:
                    fill(h_ref, k - 6, side * 9, z, up, down)

    lane = lax.broadcasted_iota(jnp.int32, (EXT, ROW), 1)
    first, last = lane == 0, lane == ROW - 1
    row = lax.broadcasted_iota(jnp.int32, (EXT, ROW), 0)
    inside = jnp.where((row == 32) & (b_id == b_last), 0.0, 1.0) * jnp.where(
        (row == 39) & (b_id == 0), 0.0, 1.0
    )

    def get(ref, c, layer):
        return ref[c, layer, 0], ref[c, layer, 1]

    def smooth(below, mid, above):
        t = add(add(below, mid), add(mid, above))
        t = add(t, y_next(t))
        t = own(add(t, y_prev(t)))
        return add(add(t, t), add(z_prev(t, first, 0.0), z_next(t, last, 0.0)))

    def strain_layer(i, _):
        u = [get(v_ref, c, i + 1) for c in range(3)]
        keep = jnp.where(((i == 0) & (a_id == 0)) | ((i == 9) & (a_id == a_last)), 0.0, 1.0)
        m = inside * keep
        gx = [sub(get(v_ref, c, i + 2), get(v_ref, c, i)) for c in range(3)]
        gy = [sub(y_next(p), y_prev(p)) for p in u]
        gz = [sub(z_next(p, last, 0.0), z_prev(p, first, 0.0)) for p in u]
        t = [
            add(gx[0], gx[0]),
            add(gy[1], gy[1]),
            add(gz[2], gz[2]),
            add(gy[0], gx[1]),
            add(gz[0], gx[2]),
            add(gz[1], gy[2]),
        ]
        t = [each(lambda p: p * m, p) for p in t]
        q = [mul(p, p) for p in t]
        diag = add(add(q[0], q[1]), q[2])
        off = add(add(q[3], q[4]), q[5])
        mag = each(lambda p, r: jnp.sqrt((p + 2.0 * r) * 0.125), diag, off)

        @pl.when((i >= 1) & (i <= 8))
        def _():
            for z, cols in enumerate(halves):
                mag_ref[i - 1, :, cols] = mag[z][:NYL]

        for c in range(6):
            w = mul(mag, t[c])
            uu = mul(u[PAIRS[c][0]], u[PAIRS[c][1]])
            for z in range(2):
                s_ref[c, i, z] = t[c][z]
                s_ref[6 + c, i, z] = w[z]
                s_ref[12 + c, i, z] = uu[z]
        return 0

    lax.fori_loop(0, 10, strain_layer, 0)

    def close_layer(x, _):
        def hat(ref, c, at):
            return smooth(get(ref, c, at), get(ref, c, at + 1), get(ref, c, at + 2))

        s = [hat(s_ref, c, x) for c in range(6)]
        q = [mul(p, p) for p in s]
        diag = add(add(q[0], q[1]), q[2])
        off = add(add(q[3], q[4]), q[5])
        smag4 = each(lambda p, r: jnp.sqrt((p + 2.0 * r) * 0.125) * (4.0 / 64.0), diag, off)
        uh = [each(lambda p: p * (1.0 / 64.0), hat(v_ref, c, x + 1)) for c in range(3)]
        lm = mm = None
        for c in range(6):
            ms = hat(s_ref, 6 + c, x)
            m = each(lambda p, r, g: (p - g * r) * (1.0 / 128.0), ms, s[c], smag4)
            uu = hat(s_ref, 12 + c, x)
            ll = each(
                lambda p, r, g: p * (1.0 / 64.0) - r * g, uu, uh[PAIRS[c][0]], uh[PAIRS[c][1]]
            )
            m2 = m if c < 3 else add(m, m)
            dl, dm = mul(ll, m2), mul(m, m2)
            lm = dl if lm is None else add(lm, dl)
            mm = dm if mm is None else add(mm, dm)

        speed = [each(lambda p: DT * p, get(v_ref, c, x + 2)) for c in range(3)]
        moved = []
        for f in range(2):
            g = get(h_ref, f, x + 1)
            lower, upper = get(h_ref, f, x), get(h_ref, f, x + 2)

            def carry(mid, low, up, sp):
                return each(
                    lambda p, lo, hi, v: p + jnp.abs(v) * (jnp.where(v > 0, lo, hi) - p),
                    mid, low, up, sp,
                )

            g = carry(g, lower, upper, speed[0])
            g = carry(own(g), own(y_prev(g)), own(y_next(g)), own(speed[1]))
            g = carry(g, z_prev(g, first, 0.0), z_next(g, last, 0.0), own(speed[2]))
            moved.append(g)
        k = DT / 1.5
        for z, cols in enumerate(halves):
            m0, m1 = moved[0][z], moved[1][z]
            r = lax.rsqrt(lax.rsqrt(lax.rsqrt(m0 * m1)))
            blend = k / (r + k)
            hit = hit_ref[z, pl.ds(pl.multiple_of(x * NYL, NYL), NYL), :] > 0.5
            new_lm = jnp.maximum(m0 + blend * (lm[z] - m0), 0.0)
            new_mm = m1 + blend * (mm[z] - m1)
            new_ref[0, x, :, cols] = jnp.where(hit, 0.0, new_lm)
            new_ref[1, x, :, cols] = jnp.where(hit, 0.0, new_mm)
        return 0

    lax.fori_loop(0, NXL, close_layer, 0)


def stencil(vel, hist, xl, xr, below, above, dest, weight):
    return pl.pallas_call(
        stencil_kernel,
        in_specs=[pl.BlockSpec(memory_space=pl.ANY)] * 4 + in_vmem(2) + [pl.BlockSpec(memory_space=pl.ANY)] * 2,
        out_specs=in_vmem(3),
        out_shape=[
            jax.ShapeDtypeStruct((2, NXL, NYL, NZ), F32),
            jax.ShapeDtypeStruct((NXL, NYL, NZ), F32),
            jax.ShapeDtypeStruct((8 + PEERS, ROW), F32),
        ],
        scratch_shapes=[
            pltpu.VMEM((3, 12, 2, EXT, ROW), F32),
            pltpu.VMEM((2, 10, 2, EXT, ROW), F32),
            pltpu.VMEM((18, 10, 2, EXT, ROW), F32),
            pltpu.VMEM((2, 32, NZ), F32),
            pltpu.VMEM((2, ROWS // 2, ROW), F32),
            pltpu.VMEM((CAP, PEERS), jnp.int32),
            pltpu.VMEM((CAP, PEERS), F32),
            pltpu.SemaphoreType.DMA((40,)),
        ],
        compiler_params=params(16),
        name="stencil",
        cost_estimate=pl.CostEstimate(
            flops=STENCIL_COST, transcendentals=500_000, bytes_accessed=20_000_000
        ),
    )(vel, hist, xl, xr, below, above, dest, weight)


def place_kernel(new_ref, mag_ref, table_ref, got_ref, out_hbm, eddy_hbm, out_ref, eddy_ref, sems):
    n = 2 * NYL
    place = jnp.concatenate([table_ref[0:1, :], table_ref[1:2, :]], axis=1)
    rows = lax.broadcasted_iota(jnp.int32, (2 * n, CAP * PEERS), 0)
    rows = (rows + jnp.where(rows >= n, ROWS // 2 - n, 0)).astype(F32)
    blended = []
    for c in range(CAP):
        wc = table_ref[8:, c : c + 1]
        cols = []
        for f in range(2):
            r0, r1 = got_ref[:, f * 4 + c * 2, :], got_ref[:, f * 4 + c * 2 + 1, :]
            cols.append(wc * r0 + (1.0 - wc) * r1)
        blended.append(jnp.concatenate(cols, axis=1))
    parts = split3(jnp.concatenate(blended, axis=0))
    copies = []
    for stage in range(NXL // 2):
        onehot = jnp.where(rows + float(stage * n) == place, 1.0, 0.0).astype(BF16)
        acc = None
        for part in parts:
            d = jnp.dot(onehot, part, preferred_element_type=F32)
            acc = d if acc is None else acc + d
        layers = slice(stage * 2, stage * 2 + 2)
        at = pl.ds(stage * 2, 2)
        for h in range(2):
            cols = slice(h * ROW, (h + 1) * ROW)
            final = []
            for f in range(2):
                cur = new_ref[f, layers, :, cols].reshape(n, ROW)
                val = cur + acc[h * n : (h + 1) * n, f * ROW : (f + 1) * ROW]
                out_ref[f, layers, :, cols] = val.reshape(2, NYL, ROW)
                final.append(val)
            eddy = final[0] / final[1] * mag_ref[layers, :, cols].reshape(n, ROW)
            eddy_ref[layers, :, cols] = eddy.reshape(2, NYL, ROW)
        copies.append(
            pltpu.make_async_copy(out_ref.at[:, at], out_hbm.at[:, at], sems.at[0, stage])
        )
        copies.append(pltpu.make_async_copy(eddy_ref.at[at], eddy_hbm.at[at], sems.at[1, stage]))
        copies[-2].start()
        copies[-1].start()
    for copy in copies:
        copy.wait()


def place_rows(new, mag, table, got):
    return pl.pallas_call(
        place_kernel,
        in_specs=in_vmem(4),
        out_specs=[pl.BlockSpec(memory_space=pl.ANY)] * 2,
        out_shape=[
            jax.ShapeDtypeStruct((2, NXL, NYL, NZ), F32),
            jax.ShapeDtypeStruct((NXL, NYL, NZ), F32),
        ],
        scratch_shapes=[
            pltpu.VMEM((2, NXL, NYL, NZ), F32),
            pltpu.VMEM((NXL, NYL, NZ), F32),
            pltpu.SemaphoreType.DMA((2, 4)),
        ],
        compiler_params=params(12),
        name="place_receptors",
        cost_estimate=pl.CostEstimate(
            flops=300_000_000, transcendentals=100_000, bytes_accessed=2_500_000
        ),
    )(new, mag, table, got)


def body(velocity, history, donor_rows, recv_dest, recv_weight):
    vel, hist = velocity[:, 0], history[:, 0]
    idx = jnp.transpose(donor_rows[0, 0, 0], (1, 2, 0)).reshape(2 * CAP, PEERS)

    up, down = edges(vel, hist)
    below = shift_ring(up, "span", 1)
    above = shift_ring(down, "span", -1)

    chosen = gather(hist, idx)
    chosen = lax.ppermute(chosen, "grid", [(0, 1), (1, 0)])
    chosen = chosen.reshape(PEERS, 1, 8 * ROW)
    got = lax.all_to_all(chosen, ("stream", "span"), split_axis=0, concat_axis=0, tiled=True)
    got = got.reshape(PEERS, 8, ROW)

    right, left = faces(vel, hist, below, above)
    xl = shift_ring(right, "stream", 1)
    xr = shift_ring(left, "stream", -1)
    dest = jnp.transpose(recv_dest[0, 0, 0])
    weight = jnp.transpose(recv_weight[0, 0, 0])
    made = stencil(vel, hist, xl, xr, below, above, dest, weight)
    final, eddy = place_rows(*made, got)
    return final[:, None], eddy[None]


def solution(mesh):
    in_specs = (
        P(None, "grid", "stream", "span", None),
        P(None, "grid", "stream", "span", None),
        P("grid", "stream", "span", None, None, None),
        P("grid", "stream", "span", None, None),
        P("grid", "stream", "span", None, None),
    )
    out_specs = (P(None, "grid", "stream", "span", None), P("grid", "stream", "span", None))
    return jax.shard_map(body, mesh=mesh, in_specs=in_specs, out_specs=out_specs, check_vma=False)
```

```python
import jax
import jax.numpy as jnp
from jax import lax
from jax.experimental import pallas as pl
from jax.experimental.pallas import tpu as pltpu
from jax.sharding import PartitionSpec as P

F32 = jnp.float32
BF16 = jnp.bfloat16
NXL, NYL, NZ, ROW = 8, 32, 256, 128
ROWS = 512
PEERS = 128
CAP = 2
FACE = 8 * NYL
EDGE_ROOM = 10500 * 1024
FACE_COST = 10_000_000_000
STENCIL_COST = 10_000_000_000
EXT = 40
DT = 0.2
MIB = 1024 * 1024
PAIRS = ((0, 0), (1, 1), (2, 2), (0, 1), (0, 2), (1, 2))


def in_vmem(n):
    return [pl.BlockSpec(memory_space=pltpu.VMEM)] * n


def params(mib):
    return pltpu.CompilerParams(vmem_limit_bytes=mib * MIB)


def shift_ring(x, axis, step):
    n = lax.axis_size(axis)
    return lax.ppermute(x, axis, [(i, (i + step) % n) for i in range(n)])


def split3(x):
    hi = x.astype(BF16)
    rest = x - hi.astype(F32)
    mid = rest.astype(BF16)
    low = (rest - mid.astype(F32)).astype(BF16)
    return hi, mid, low


def gather_kernel(hist_ref, idx_hbm, out_ref, idx_ref, sem):
    copy = pltpu.make_async_copy(idx_hbm, idx_ref, sem)
    copy.start()
    halves = []
    for h in range(2):
        cols = [
            hist_ref[f, :, :, h * ROW : (h + 1) * ROW].reshape(NXL * NYL, ROW)
            for f in range(2)
        ]
        halves.extend(split3(jnp.concatenate(cols, axis=1)))
    table = jnp.concatenate(halves, axis=0)
    copy.wait()
    idx = idx_ref[...]
    place = (idx % 2) * (ROWS // 2) + idx // 2
    place = jnp.transpose(jnp.concatenate([place, place], axis=0).astype(F32))
    lanes = lax.broadcasted_iota(jnp.int32, (PEERS, ROWS // 2), 1).astype(F32)
    for j in range(2 * CAP):
        col = place[:, j : j + 1]
        onehots = []
        for h in range(2):
            onehot = jnp.where(lanes + float(h * ROWS // 2) == col, 1.0, 0.0).astype(BF16)
            onehots += [onehot] * 3
        acc = jnp.dot(jnp.concatenate(onehots, axis=1), table, preferred_element_type=F32)
        for f in range(2):
            out_ref[:, f * 4 + j, :] = acc[:, f * ROW : (f + 1) * ROW]


def gather(hist, idx):
    return pl.pallas_call(
        gather_kernel,
        in_specs=in_vmem(1) + [pl.BlockSpec(memory_space=pl.ANY)],
        out_specs=in_vmem(1)[0],
        scratch_shapes=[
            pltpu.VMEM((2 * CAP, PEERS), jnp.int32),
            pltpu.SemaphoreType.DMA(()),
        ],
        out_shape=jax.ShapeDtypeStruct((PEERS, 8, ROW), F32),
        compiler_params=params(8),
        name="pick_donors",
        cost_estimate=pl.CostEstimate(
            flops=400_000_000, transcendentals=0, bytes_accessed=1_100_000
        ),
    )(hist, idx)


def edge_kernel(vel_hbm, his_hbm, up_ref, down_ref, sems):
    copies = []
    for side, (out, v_row, h_row) in enumerate(
        ((up_ref, NYL - 2, NYL - 1), (down_ref, 0, 0))
    ):
        for c in range(3):
            copies.append(
                pltpu.make_async_copy(
                    vel_hbm.at[c, :, pl.ds(v_row, 2), :],
                    out.at[:, pl.ds(2 * c, 2), :],
                    sems.at[side, c],
                )
            )
        for f in range(2):
            copies.append(
                pltpu.make_async_copy(
                    his_hbm.at[f, :, pl.ds(h_row, 1), :],
                    out.at[:, pl.ds(6 + f, 1), :],
                    sems.at[side, 3 + f],
                )
            )
    for copy in copies:
        copy.start()
    for copy in copies:
        copy.wait()


def edges(vel, hist):
    shape = jax.ShapeDtypeStruct((NXL, 8, NZ), F32)
    return pl.pallas_call(
        edge_kernel,
        in_specs=[pl.BlockSpec(memory_space=pl.ANY)] * 2,
        out_specs=in_vmem(2),
        out_shape=[shape, shape],
        scratch_shapes=[
            pltpu.SemaphoreType.DMA((2, 5)),
        ],
        compiler_params=pltpu.CompilerParams(vmem_limit_bytes=64 * MIB - EDGE_ROOM),
        name="edge_rows",
        cost_estimate=pl.CostEstimate(flops=100_000, transcendentals=0, bytes_accessed=1_000_000),
    )(vel, hist)


def span_keeps():
    b = lax.axis_index("span")
    keep_above = jnp.where(b == lax.axis_size("span") - 1, 0.0, 1.0)
    return jnp.where(b == 0, 0.0, 1.0), keep_above


def face_kernel(vel_ref, his_ref, below_ref, above_ref, right_ref, left_ref):
    a = lax.axis_index("stream")
    last = lax.axis_size("stream") - 1
    keep_below, keep_above = span_keeps()
    for out_ref, first, hist_layer, keep in (
        (right_ref, NXL - 2, NXL - 1, jnp.where(a == last, 0.0, 1.0)),
        (left_ref, 0, 0, jnp.where(a == 0, 0.0, 1.0)),
    ):
        for k in range(8):
            if k < 6:
                c, layer = k // 2, first + k % 2
                plane = vel_ref[c, layer]
                rows = slice(c * 2, c * 2 + 2)
                up, down = above_ref[layer, rows, :], below_ref[layer, rows, :]
            else:
                layer = hist_layer
                plane = his_ref[k - 6, layer]
                up, down = above_ref[layer, k : k + 1, :], below_ref[layer, k : k + 1, :]
            out_ref[k * NYL : (k + 1) * NYL, :] = plane * keep
            base, n = FACE + 4 * k, up.shape[0]
            out_ref[base : base + n, :] = up * (keep * keep_above)
            out_ref[base + 4 - n : base + 4, :] = down * (keep * keep_below)
            if n == 1:
                out_ref[base + 1 : base + 3, :] = jnp.zeros((2, NZ), F32)


def faces(vel, hist, below, above):
    shape = jax.ShapeDtypeStruct((FACE + 32, NZ), F32)
    return pl.pallas_call(
        face_kernel,
        in_specs=in_vmem(4),
        out_specs=in_vmem(2),
        out_shape=[shape, shape],
        compiler_params=params(4),
        name="face_layers",
        cost_estimate=pl.CostEstimate(flops=FACE_COST, transcendentals=0, bytes_accessed=1_200_000),
    )(vel, hist, below, above)


def add(a, b):
    return tuple(p + q for p, q in zip(a, b))


def sub(a, b):
    return tuple(p - q for p, q in zip(a, b))


def mul(a, b):
    return tuple(p * q for p, q in zip(a, b))


def each(fn, *a):
    return tuple(fn(*p) for p in zip(*a))


def y_next(a):
    return tuple(pltpu.roll(p, EXT - 1, 0) for p in a)


def y_prev(a):
    return tuple(pltpu.roll(p, 1, 0) for p in a)


def own(a):
    return tuple(p[:NYL] for p in a)


def z_prev(a, first, fill):
    lo, hi = a
    rlo, rhi = pltpu.roll(lo, 1, 1), pltpu.roll(hi, 1, 1)
    m = first[: lo.shape[0]]
    return jnp.where(m, fill, rlo), jnp.where(m, rlo, rhi)


def z_next(a, last, fill):
    lo, hi = a
    rlo, rhi = pltpu.roll(lo, ROW - 1, 1), pltpu.roll(hi, ROW - 1, 1)
    m = last[: lo.shape[0]]
    return jnp.where(m, rhi, rlo), jnp.where(m, fill, rhi)


def placement(dest_ref, w_ref, table_ref, hit_ref):
    dest = dest_ref[...]
    place = jnp.where(dest >= ROWS, -1, (dest % 2) * (ROWS // 2) + dest // 2).astype(F32)
    for c in range(CAP):
        table_ref[c : c + 1, :] = place[c : c + 1]
    table_ref[8:, :] = jnp.zeros((PEERS, ROW), F32)
    table_ref[8:, 0:8] = jnp.transpose(jnp.concatenate([w_ref[...]] * 4, axis=0))
    ones = jnp.ones((CAP * PEERS, ROW), BF16)
    place = jnp.concatenate([place[0:1], place[1:2]], axis=1)
    rows = lax.broadcasted_iota(jnp.int32, (ROWS // 2, CAP * PEERS), 0).astype(F32)
    for h in range(2):
        onehot = jnp.where(rows + float(h * ROWS // 2) == place, 1.0, 0.0).astype(BF16)
        hit_ref[h] = jnp.dot(onehot, ones, preferred_element_type=F32)


def stencil_kernel(
    vel_hbm, his_hbm, xl_hbm, xr_hbm, below_ref, above_ref, dest_hbm, w_hbm,
    new_ref, mag_ref, table_ref,
    v_ref, h_ref, s_ref, corner_ref, hit_ref, dest_ref, w_ref, sems,
):
    a_id = lax.axis_index("stream")
    b_id = lax.axis_index("span")
    a_last = lax.axis_size("stream") - 1
    b_last = lax.axis_size("span") - 1
    halves = (slice(0, ROW), slice(ROW, NZ))

    copies = [
        pltpu.make_async_copy(
            ref.at[pl.ds(FACE, 32), :], corner_ref.at[side], sems.at[side]
        )
        for side, ref in enumerate((xl_hbm, xr_hbm))
    ]
    copies.append(pltpu.make_async_copy(dest_hbm, dest_ref, sems.at[38]))
    copies.append(pltpu.make_async_copy(w_hbm, w_ref, sems.at[39]))
    for z, cols in enumerate(halves):
        lanes = pl.ds(z * ROW, ROW)
        copies.append(
            pltpu.make_async_copy(
                vel_hbm.at[:, :, :, lanes],
                v_ref.at[:, pl.ds(2, NXL), z, pl.ds(0, NYL), :],
                sems.at[2 + z],
            )
        )
        copies.append(
            pltpu.make_async_copy(
                his_hbm.at[:, :, :, lanes],
                h_ref.at[:, pl.ds(1, NXL), z, pl.ds(0, NYL), :],
                sems.at[4 + z],
            )
        )
        for side, ref in enumerate((xl_hbm, xr_hbm)):
            for k in range(8):
                rows = pl.ds(k * NYL, NYL)
                if k < 6:
                    to = v_ref.at[k // 2, side * 10 + k % 2, z, pl.ds(0, NYL), :]
                else:
                    to = h_ref.at[k - 6, side * 9, z, pl.ds(0, NYL), :]
                copies.append(
                    pltpu.make_async_copy(
                        ref.at[rows, lanes], to, sems.at[6 + (side * 2 + z) * 8 + k]
                    )
                )
    for copy in copies:
        copy.start()

    zero4 = jnp.zeros((4, ROW), F32)
    keep_below, keep_above = span_keeps()

    def fill(ref, c, layer, z, up, down):
        n = up.shape[0]
        ref[c, layer, z, NYL : NYL + n, :] = up
        ref[c, layer, z, NYL + n : NYL + n + 4, :] = zero4
        ref[c, layer, z, NYL + 4 : EXT - n, :] = zero4[: 4 - n]
        ref[c, layer, z, EXT - n :, :] = down

    for z, cols in enumerate(halves):
        for layer in range(NXL):
            for c in range(3):
                rows = slice(c * 2, c * 2 + 2)
                up = above_ref[layer, rows, cols] * keep_above
                down = below_ref[layer, rows, cols] * keep_below
                fill(v_ref, c, layer + 2, z, up, down)
            for f in range(2):
                rows = slice(6 + f, 7 + f)
                up = above_ref[layer, rows, cols] * keep_above
                down = below_ref[layer, rows, cols] * keep_below
                fill(h_ref, f, layer + 1, z, up, down)
    for copy in copies:
        copy.wait()
    placement(dest_ref, w_ref, table_ref, hit_ref)
    for z, cols in enumerate(halves):
        for side in range(2):
            for k in range(8):
                n = 2 if k < 6 else 1
                up = corner_ref[side, 4 * k : 4 * k + n, cols]
                down = corner_ref[side, 4 * k + 4 - n : 4 * k + 4, cols]
                if k < 6:
                    fill(v_ref, k // 2, side * 10 + k % 2, z, up, down)
                else:
                    fill(h_ref, k - 6, side * 9, z, up, down)

    lane = lax.broadcasted_iota(jnp.int32, (EXT, ROW), 1)
    first, last = lane == 0, lane == ROW - 1
    row = lax.broadcasted_iota(jnp.int32, (EXT, ROW), 0)
    inside = jnp.where((row == 32) & (b_id == b_last), 0.0, 1.0) * jnp.where(
        (row == 39) & (b_id == 0), 0.0, 1.0
    )

    def get(ref, c, layer):
        return ref[c, layer, 0], ref[c, layer, 1]

    def smooth(below, mid, above):
        t = add(add(below, mid), add(mid, above))
        t = add(t, y_next(t))
        t = own(add(t, y_prev(t)))
        return add(add(t, t), add(z_prev(t, first, 0.0), z_next(t, last, 0.0)))

    def strain_layer(i, _):
        u = [get(v_ref, c, i + 1) for c in range(3)]
        keep = jnp.where(((i == 0) & (a_id == 0)) | ((i == 9) & (a_id == a_last)), 0.0, 1.0)
        m = inside * keep
        gx = [sub(get(v_ref, c, i + 2), get(v_ref, c, i)) for c in range(3)]
        gy = [sub(y_next(p), y_prev(p)) for p in u]
        gz = [sub(z_next(p, last, 0.0), z_prev(p, first, 0.0)) for p in u]
        t = [
            add(gx[0], gx[0]),
            add(gy[1], gy[1]),
            add(gz[2], gz[2]),
            add(gy[0], gx[1]),
            add(gz[0], gx[2]),
            add(gz[1], gy[2]),
        ]
        t = [each(lambda p: p * m, p) for p in t]
        q = [mul(p, p) for p in t]
        diag = add(add(q[0], q[1]), q[2])
        off = add(add(q[3], q[4]), q[5])
        mag = each(lambda p, r: jnp.sqrt((p + 2.0 * r) * 0.125), diag, off)

        @pl.when((i >= 1) & (i <= 8))
        def _():
            for z, cols in enumerate(halves):
                mag_ref[i - 1, :, cols] = mag[z][:NYL]

        for c in range(6):
            w = mul(mag, t[c])
            uu = mul(u[PAIRS[c][0]], u[PAIRS[c][1]])
            for z in range(2):
                s_ref[c, i, z] = t[c][z]
                s_ref[6 + c, i, z] = w[z]
                s_ref[12 + c, i, z] = uu[z]
        return 0

    lax.fori_loop(0, 10, strain_layer, 0)

    def close_layer(x, _):
        def hat(ref, c, at):
            return smooth(get(ref, c, at), get(ref, c, at + 1), get(ref, c, at + 2))

        s = [hat(s_ref, c, x) for c in range(6)]
        q = [mul(p, p) for p in s]
        diag = add(add(q[0], q[1]), q[2])
        off = add(add(q[3], q[4]), q[5])
        smag4 = each(lambda p, r: jnp.sqrt((p + 2.0 * r) * 0.125) * (4.0 / 64.0), diag, off)
        uh = [each(lambda p: p * (1.0 / 64.0), hat(v_ref, c, x + 1)) for c in range(3)]
        lm = mm = None
        for c in range(6):
            ms = hat(s_ref, 6 + c, x)
            m = each(lambda p, r, g: (p - g * r) * (1.0 / 128.0), ms, s[c], smag4)
            uu = hat(s_ref, 12 + c, x)
            ll = each(
                lambda p, r, g: p * (1.0 / 64.0) - r * g, uu, uh[PAIRS[c][0]], uh[PAIRS[c][1]]
            )
            m2 = m if c < 3 else add(m, m)
            dl, dm = mul(ll, m2), mul(m, m2)
            lm = dl if lm is None else add(lm, dl)
            mm = dm if mm is None else add(mm, dm)

        speed = [each(lambda p: DT * p, get(v_ref, c, x + 2)) for c in range(3)]
        moved = []
        for f in range(2):
            g = get(h_ref, f, x + 1)
            lower, upper = get(h_ref, f, x), get(h_ref, f, x + 2)

            def carry(mid, low, up, sp):
                return each(
                    lambda p, lo, hi, v: p + jnp.abs(v) * (jnp.where(v > 0, lo, hi) - p),
                    mid, low, up, sp,
                )

            g = carry(g, lower, upper, speed[0])
            g = carry(own(g), own(y_prev(g)), own(y_next(g)), own(speed[1]))
            g = carry(g, z_prev(g, first, 0.0), z_next(g, last, 0.0), own(speed[2]))
            moved.append(g)
        k = DT / 1.5
        for z, cols in enumerate(halves):
            m0, m1 = moved[0][z], moved[1][z]
            r = lax.rsqrt(lax.rsqrt(lax.rsqrt(m0 * m1)))
            blend = k / (r + k)
            hit = hit_ref[z, pl.ds(pl.multiple_of(x * NYL, NYL), NYL), :] > 0.5
            new_lm = jnp.maximum(m0 + blend * (lm[z] - m0), 0.0)
            new_mm = m1 + blend * (mm[z] - m1)
            new_ref[0, x, :, cols] = jnp.where(hit, 0.0, new_lm)
            new_ref[1, x, :, cols] = jnp.where(hit, 0.0, new_mm)
        return 0

    lax.fori_loop(0, NXL, close_layer, 0)


def stencil(vel, hist, xl, xr, below, above, dest, weight):
    return pl.pallas_call(
        stencil_kernel,
        in_specs=[pl.BlockSpec(memory_space=pl.ANY)] * 4 + in_vmem(2) + [pl.BlockSpec(memory_space=pl.ANY)] * 2,
        out_specs=in_vmem(3),
        out_shape=[
            jax.ShapeDtypeStruct((2, NXL, NYL, NZ), F32),
            jax.ShapeDtypeStruct((NXL, NYL, NZ), F32),
            jax.ShapeDtypeStruct((8 + PEERS, ROW), F32),
        ],
        scratch_shapes=[
            pltpu.VMEM((3, 12, 2, EXT, ROW), F32),
            pltpu.VMEM((2, 10, 2, EXT, ROW), F32),
            pltpu.VMEM((18, 10, 2, EXT, ROW), F32),
            pltpu.VMEM((2, 32, NZ), F32),
            pltpu.VMEM((2, ROWS // 2, ROW), F32),
            pltpu.VMEM((CAP, PEERS), jnp.int32),
            pltpu.VMEM((CAP, PEERS), F32),
            pltpu.SemaphoreType.DMA((40,)),
        ],
        compiler_params=params(16),
        name="stencil",
        cost_estimate=pl.CostEstimate(
            flops=STENCIL_COST, transcendentals=500_000, bytes_accessed=20_000_000
        ),
    )(vel, hist, xl, xr, below, above, dest, weight)


def place_kernel(new_ref, mag_ref, table_ref, got_ref, out_hbm, eddy_hbm, out_ref, eddy_ref, sems):
    n = 2 * NYL
    place = jnp.concatenate([table_ref[0:1, :], table_ref[1:2, :]], axis=1)
    rows = lax.broadcasted_iota(jnp.int32, (2 * n, CAP * PEERS), 0)
    rows = (rows + jnp.where(rows >= n, ROWS // 2 - n, 0)).astype(F32)
    blended = []
    for c in range(CAP):
        wc = table_ref[8:, c : c + 1]
        cols = []
        for f in range(2):
            r0, r1 = got_ref[:, f * 4 + c * 2, :], got_ref[:, f * 4 + c * 2 + 1, :]
            cols.append(wc * r0 + (1.0 - wc) * r1)
        blended.append(jnp.concatenate(cols, axis=1))
    parts = jnp.concatenate(split3(jnp.concatenate(blended, axis=0)), axis=0)
    copies = []
    for stage in range(NXL // 2):
        onehot = jnp.where(rows + float(stage * n) == place, 1.0, 0.0).astype(BF16)
        acc = jnp.dot(
            jnp.concatenate([onehot] * 3, axis=1), parts, preferred_element_type=F32
        )
        layers = slice(stage * 2, stage * 2 + 2)
        at = pl.ds(stage * 2, 2)
        for h in range(2):
            cols = slice(h * ROW, (h + 1) * ROW)
            final = []
            for f in range(2):
                cur = new_ref[f, layers, :, cols].reshape(n, ROW)
                val = cur + acc[h * n : (h + 1) * n, f * ROW : (f + 1) * ROW]
                out_ref[f, layers, :, cols] = val.reshape(2, NYL, ROW)
                final.append(val)
            eddy = final[0] / final[1] * mag_ref[layers, :, cols].reshape(n, ROW)
            eddy_ref[layers, :, cols] = eddy.reshape(2, NYL, ROW)
        copies.append(
            pltpu.make_async_copy(out_ref.at[:, at], out_hbm.at[:, at], sems.at[0, stage])
        )
        copies.append(pltpu.make_async_copy(eddy_ref.at[at], eddy_hbm.at[at], sems.at[1, stage]))
        copies[-2].start()
        copies[-1].start()
    for copy in copies:
        copy.wait()


def place_rows(new, mag, table, got):
    return pl.pallas_call(
        place_kernel,
        in_specs=in_vmem(4),
        out_specs=[pl.BlockSpec(memory_space=pl.ANY)] * 2,
        out_shape=[
            jax.ShapeDtypeStruct((2, NXL, NYL, NZ), F32),
            jax.ShapeDtypeStruct((NXL, NYL, NZ), F32),
        ],
        scratch_shapes=[
            pltpu.VMEM((2, NXL, NYL, NZ), F32),
            pltpu.VMEM((NXL, NYL, NZ), F32),
            pltpu.SemaphoreType.DMA((2, 4)),
        ],
        compiler_params=params(12),
        name="place_receptors",
        cost_estimate=pl.CostEstimate(
            flops=300_000_000, transcendentals=100_000, bytes_accessed=2_500_000
        ),
    )(new, mag, table, got)


def body(velocity, history, donor_rows, recv_dest, recv_weight):
    vel, hist = velocity[:, 0], history[:, 0]
    idx = jnp.transpose(donor_rows[0, 0, 0], (1, 2, 0)).reshape(2 * CAP, PEERS)

    up, down = edges(vel, hist)
    below = shift_ring(up, "span", 1)
    above = shift_ring(down, "span", -1)

    chosen = gather(hist, idx)
    chosen = lax.ppermute(chosen, "grid", [(0, 1), (1, 0)])
    chosen = chosen.reshape(PEERS, 1, 8 * ROW)
    got = lax.all_to_all(chosen, ("stream", "span"), split_axis=0, concat_axis=0, tiled=True)
    got = got.reshape(PEERS, 8, ROW)

    right, left = faces(vel, hist, below, above)
    xl = shift_ring(right, "stream", 1)
    xr = shift_ring(left, "stream", -1)
    dest = jnp.transpose(recv_dest[0, 0, 0])
    weight = jnp.transpose(recv_weight[0, 0, 0])
    made = stencil(vel, hist, xl, xr, below, above, dest, weight)
    final, eddy = place_rows(*made, got)
    return final[:, None], eddy[None]


def solution(mesh):
    in_specs = (
        P(None, "grid", "stream", "span", None),
        P(None, "grid", "stream", "span", None),
        P("grid", "stream", "span", None, None, None),
        P("grid", "stream", "span", None, None),
        P("grid", "stream", "span", None, None),
    )
    out_specs = (P(None, "grid", "stream", "span", None), P("grid", "stream", "span", None))
    return jax.shard_map(body, mesh=mesh, in_specs=in_specs, out_specs=out_specs, check_vma=False)
```

```python
import jax
import jax.numpy as jnp
from jax import lax
from jax.experimental import pallas as pl
from jax.experimental.pallas import tpu as pltpu
from jax.sharding import PartitionSpec as P

F32 = jnp.float32
BF16 = jnp.bfloat16
NXL, NYL, NZ, ROW = 8, 32, 256, 128
ROWS = 512
PEERS = 128
CAP = 2
FACE = 8 * NYL
EDGE_ROOM = 10500 * 1024
FACE_COST = 10_000_000_000
STENCIL_COST = 10_000_000_000
EXT = 40
DT = 0.2
MIB = 1024 * 1024
PAIRS = ((0, 0), (1, 1), (2, 2), (0, 1), (0, 2), (1, 2))


def in_vmem(n):
    return [pl.BlockSpec(memory_space=pltpu.VMEM)] * n


def params(mib):
    return pltpu.CompilerParams(vmem_limit_bytes=mib * MIB)


def shift_ring(x, axis, step):
    n = lax.axis_size(axis)
    return lax.ppermute(x, axis, [(i, (i + step) % n) for i in range(n)])


def split3(x):
    hi = x.astype(BF16)
    rest = x - hi.astype(F32)
    mid = rest.astype(BF16)
    low = (rest - mid.astype(F32)).astype(BF16)
    return hi, mid, low


def gather_kernel(hist_ref, idx_hbm, out_ref, idx_ref, sem):
    copy = pltpu.make_async_copy(idx_hbm, idx_ref, sem)
    copy.start()
    halves = []
    for h in range(2):
        cols = [
            hist_ref[f, :, :, h * ROW : (h + 1) * ROW].reshape(NXL * NYL, ROW)
            for f in range(2)
        ]
        halves.extend(split3(jnp.concatenate(cols, axis=1)))
    table = jnp.concatenate(halves, axis=0)
    copy.wait()
    idx = idx_ref[...]
    place = (idx % 2) * (ROWS // 2) + idx // 2
    place = jnp.transpose(jnp.concatenate([place, place], axis=0).astype(F32))
    lanes = lax.broadcasted_iota(jnp.int32, (PEERS, ROWS // 2), 1).astype(F32)
    for j in range(2 * CAP):
        col = place[:, j : j + 1]
        onehots = []
        for h in range(2):
            onehot = jnp.where(lanes + float(h * ROWS // 2) == col, 1.0, 0.0).astype(BF16)
            onehots += [onehot] * 3
        acc = jnp.dot(jnp.concatenate(onehots, axis=1), table, preferred_element_type=F32)
        for f in range(2):
            out_ref[:, f * 4 + j, :] = acc[:, f * ROW : (f + 1) * ROW]


def gather(hist, idx):
    return pl.pallas_call(
        gather_kernel,
        in_specs=in_vmem(1) + [pl.BlockSpec(memory_space=pl.ANY)],
        out_specs=in_vmem(1)[0],
        scratch_shapes=[
            pltpu.VMEM((2 * CAP, PEERS), jnp.int32),
            pltpu.SemaphoreType.DMA(()),
        ],
        out_shape=jax.ShapeDtypeStruct((PEERS, 8, ROW), F32),
        compiler_params=params(8),
        name="pick_donors",
        cost_estimate=pl.CostEstimate(
            flops=400_000_000, transcendentals=0, bytes_accessed=1_100_000
        ),
    )(hist, idx)


def edge_kernel(vel_hbm, his_hbm, up_ref, down_ref, sems):
    copies = []
    for side, (out, v_row, h_row) in enumerate(
        ((up_ref, NYL - 2, NYL - 1), (down_ref, 0, 0))
    ):
        for c in range(3):
            copies.append(
                pltpu.make_async_copy(
                    vel_hbm.at[c, :, pl.ds(v_row, 2), :],
                    out.at[:, pl.ds(2 * c, 2), :],
                    sems.at[side, c],
                )
            )
        for f in range(2):
            copies.append(
                pltpu.make_async_copy(
                    his_hbm.at[f, :, pl.ds(h_row, 1), :],
                    out.at[:, pl.ds(6 + f, 1), :],
                    sems.at[side, 3 + f],
                )
            )
    for copy in copies:
        copy.start()
    for copy in copies:
        copy.wait()


def edges(vel, hist):
    shape = jax.ShapeDtypeStruct((NXL, 8, NZ), F32)
    return pl.pallas_call(
        edge_kernel,
        in_specs=[pl.BlockSpec(memory_space=pl.ANY)] * 2,
        out_specs=in_vmem(2),
        out_shape=[shape, shape],
        scratch_shapes=[
            pltpu.SemaphoreType.DMA((2, 5)),
        ],
        compiler_params=pltpu.CompilerParams(vmem_limit_bytes=64 * MIB - EDGE_ROOM),
        name="edge_rows",
        cost_estimate=pl.CostEstimate(flops=100_000, transcendentals=0, bytes_accessed=1_000_000),
    )(vel, hist)


def span_keeps():
    b = lax.axis_index("span")
    keep_above = jnp.where(b == lax.axis_size("span") - 1, 0.0, 1.0)
    return jnp.where(b == 0, 0.0, 1.0), keep_above


def face_kernel(vel_ref, his_ref, below_ref, above_ref, right_ref, left_ref):
    a = lax.axis_index("stream")
    last = lax.axis_size("stream") - 1
    keep_below, keep_above = span_keeps()
    for out_ref, first, hist_layer, keep in (
        (right_ref, NXL - 2, NXL - 1, jnp.where(a == last, 0.0, 1.0)),
        (left_ref, 0, 0, jnp.where(a == 0, 0.0, 1.0)),
    ):
        for k in range(8):
            if k < 6:
                c, layer = k // 2, first + k % 2
                plane = vel_ref[c, layer]
                rows = slice(c * 2, c * 2 + 2)
                up, down = above_ref[layer, rows, :], below_ref[layer, rows, :]
            else:
                layer = hist_layer
                plane = his_ref[k - 6, layer]
                up, down = above_ref[layer, k : k + 1, :], below_ref[layer, k : k + 1, :]
            out_ref[k * NYL : (k + 1) * NYL, :] = plane * keep
            base, n = FACE + 4 * k, up.shape[0]
            out_ref[base : base + n, :] = up * (keep * keep_above)
            out_ref[base + 4 - n : base + 4, :] = down * (keep * keep_below)
            if n == 1:
                out_ref[base + 1 : base + 3, :] = jnp.zeros((2, NZ), F32)


def faces(vel, hist, below, above):
    shape = jax.ShapeDtypeStruct((FACE + 32, NZ), F32)
    return pl.pallas_call(
        face_kernel,
        in_specs=in_vmem(4),
        out_specs=in_vmem(2),
        out_shape=[shape, shape],
        compiler_params=params(4),
        name="face_layers",
        cost_estimate=pl.CostEstimate(flops=FACE_COST, transcendentals=0, bytes_accessed=1_200_000),
    )(vel, hist, below, above)


def add(a, b):
    return tuple(p + q for p, q in zip(a, b))


def sub(a, b):
    return tuple(p - q for p, q in zip(a, b))


def mul(a, b):
    return tuple(p * q for p, q in zip(a, b))


def each(fn, *a):
    return tuple(fn(*p) for p in zip(*a))


def y_next(a):
    return tuple(pltpu.roll(p, EXT - 1, 0) for p in a)


def y_prev(a):
    return tuple(pltpu.roll(p, 1, 0) for p in a)


def own(a):
    return tuple(p[:NYL] for p in a)


def z_prev(a, first, fill):
    lo, hi = a
    rlo, rhi = pltpu.roll(lo, 1, 1), pltpu.roll(hi, 1, 1)
    m = first[: lo.shape[0]]
    return jnp.where(m, fill, rlo), jnp.where(m, rlo, rhi)


def z_next(a, last, fill):
    lo, hi = a
    rlo, rhi = pltpu.roll(lo, ROW - 1, 1), pltpu.roll(hi, ROW - 1, 1)
    m = last[: lo.shape[0]]
    return jnp.where(m, rhi, rlo), jnp.where(m, fill, rhi)


def placement(dest_ref, w_ref, table_ref, hit_ref):
    dest = dest_ref[...]
    place = jnp.where(dest >= ROWS, -1, (dest % 2) * (ROWS // 2) + dest // 2).astype(F32)
    for c in range(CAP):
        table_ref[c : c + 1, :] = place[c : c + 1]
    table_ref[8:, :] = jnp.zeros((PEERS, ROW), F32)
    table_ref[8:, 0:8] = jnp.transpose(jnp.concatenate([w_ref[...]] * 4, axis=0))
    ones = jnp.ones((CAP * PEERS, ROW), BF16)
    place = jnp.concatenate([place[0:1], place[1:2]], axis=1)
    rows = lax.broadcasted_iota(jnp.int32, (ROWS // 2, CAP * PEERS), 0).astype(F32)
    for h in range(2):
        onehot = jnp.where(rows + float(h * ROWS // 2) == place, 1.0, 0.0).astype(BF16)
        hit_ref[h] = jnp.dot(onehot, ones, preferred_element_type=F32)


def stencil_kernel(
    vel_hbm, his_hbm, xl_hbm, xr_hbm, below_ref, above_ref, dest_hbm, w_hbm,
    new_ref, mag_ref, table_ref,
    v_ref, h_ref, s_ref, corner_ref, hit_ref, dest_ref, w_ref, sems,
):
    a_id = lax.axis_index("stream")
    b_id = lax.axis_index("span")
    a_last = lax.axis_size("stream") - 1
    b_last = lax.axis_size("span") - 1
    halves = (slice(0, ROW), slice(ROW, NZ))

    copies = [
        pltpu.make_async_copy(
            ref.at[pl.ds(FACE, 32), :], corner_ref.at[side], sems.at[side]
        )
        for side, ref in enumerate((xl_hbm, xr_hbm))
    ]
    copies.append(pltpu.make_async_copy(dest_hbm, dest_ref, sems.at[38]))
    copies.append(pltpu.make_async_copy(w_hbm, w_ref, sems.at[39]))
    for z, cols in enumerate(halves):
        lanes = pl.ds(z * ROW, ROW)
        copies.append(
            pltpu.make_async_copy(
                vel_hbm.at[:, :, :, lanes],
                v_ref.at[:, pl.ds(2, NXL), z, pl.ds(0, NYL), :],
                sems.at[2 + z],
            )
        )
        copies.append(
            pltpu.make_async_copy(
                his_hbm.at[:, :, :, lanes],
                h_ref.at[:, pl.ds(1, NXL), z, pl.ds(0, NYL), :],
                sems.at[4 + z],
            )
        )
        for side, ref in enumerate((xl_hbm, xr_hbm)):
            for k in range(8):
                rows = pl.ds(k * NYL, NYL)
                if k < 6:
                    to = v_ref.at[k // 2, side * 10 + k % 2, z, pl.ds(0, NYL), :]
                else:
                    to = h_ref.at[k - 6, side * 9, z, pl.ds(0, NYL), :]
                copies.append(
                    pltpu.make_async_copy(
                        ref.at[rows, lanes], to, sems.at[6 + (side * 2 + z) * 8 + k]
                    )
                )
    for copy in copies:
        copy.start()

    zero4 = jnp.zeros((4, ROW), F32)
    keep_below, keep_above = span_keeps()

    def fill(ref, c, layer, z, up, down):
        n = up.shape[0]
        ref[c, layer, z, NYL : NYL + n, :] = up
        ref[c, layer, z, NYL + n : NYL + n + 4, :] = zero4
        ref[c, layer, z, NYL + 4 : EXT - n, :] = zero4[: 4 - n]
        ref[c, layer, z, EXT - n :, :] = down

    for z, cols in enumerate(halves):
        for layer in range(NXL):
            for c in range(3):
                rows = slice(c * 2, c * 2 + 2)
                up = above_ref[layer, rows, cols] * keep_above
                down = below_ref[layer, rows, cols] * keep_below
                fill(v_ref, c, layer + 2, z, up, down)
            for f in range(2):
                rows = slice(6 + f, 7 + f)
                up = above_ref[layer, rows, cols] * keep_above
                down = below_ref[layer, rows, cols] * keep_below
                fill(h_ref, f, layer + 1, z, up, down)
    for copy in copies:
        copy.wait()
    placement(dest_ref, w_ref, table_ref, hit_ref)
    for z, cols in enumerate(halves):
        for side in range(2):
            for k in range(8):
                n = 2 if k < 6 else 1
                up = corner_ref[side, 4 * k : 4 * k + n, cols]
                down = corner_ref[side, 4 * k + 4 - n : 4 * k + 4, cols]
                if k < 6:
                    fill(v_ref, k // 2, side * 10 + k % 2, z, up, down)
                else:
                    fill(h_ref, k - 6, side * 9, z, up, down)

    lane = lax.broadcasted_iota(jnp.int32, (EXT, ROW), 1)
    first, last = lane == 0, lane == ROW - 1
    row = lax.broadcasted_iota(jnp.int32, (EXT, ROW), 0)
    inside = jnp.where((row == 32) & (b_id == b_last), 0.0, 1.0) * jnp.where(
        (row == 39) & (b_id == 0), 0.0, 1.0
    )

    def get(ref, c, layer):
        return ref[c, layer, 0], ref[c, layer, 1]

    def smooth(below, mid, above):
        t = add(add(below, mid), add(mid, above))
        t = add(t, y_next(t))
        t = own(add(t, y_prev(t)))
        return add(add(t, t), add(z_prev(t, first, 0.0), z_next(t, last, 0.0)))

    def strain_layer(i, _):
        u = [get(v_ref, c, i + 1) for c in range(3)]
        keep = jnp.where(((i == 0) & (a_id == 0)) | ((i == 9) & (a_id == a_last)), 0.0, 1.0)
        m = inside * keep
        gx = [sub(get(v_ref, c, i + 2), get(v_ref, c, i)) for c in range(3)]
        gy = [sub(y_next(p), y_prev(p)) for p in u]
        gz = [sub(z_next(p, last, 0.0), z_prev(p, first, 0.0)) for p in u]
        t = [
            add(gx[0], gx[0]),
            add(gy[1], gy[1]),
            add(gz[2], gz[2]),
            add(gy[0], gx[1]),
            add(gz[0], gx[2]),
            add(gz[1], gy[2]),
        ]
        t = [each(lambda p: p * m, p) for p in t]
        q = [mul(p, p) for p in t]
        diag = add(add(q[0], q[1]), q[2])
        off = add(add(q[3], q[4]), q[5])
        mag = each(lambda p, r: jnp.sqrt((p + 2.0 * r) * 0.125), diag, off)

        @pl.when((i >= 1) & (i <= 8))
        def _():
            for z, cols in enumerate(halves):
                mag_ref[i - 1, :, cols] = mag[z][:NYL]

        for c in range(6):
            w = mul(mag, t[c])
            uu = mul(u[PAIRS[c][0]], u[PAIRS[c][1]])
            for z in range(2):
                s_ref[c, i, z] = t[c][z]
                s_ref[6 + c, i, z] = w[z]
                s_ref[12 + c, i, z] = uu[z]
        return 0

    lax.fori_loop(0, 10, strain_layer, 0)

    def close_layer(x, _):
        def hat(ref, c, at):
            return smooth(get(ref, c, at), get(ref, c, at + 1), get(ref, c, at + 2))

        s = [hat(s_ref, c, x) for c in range(6)]
        q = [mul(p, p) for p in s]
        diag = add(add(q[0], q[1]), q[2])
        off = add(add(q[3], q[4]), q[5])
        smag4 = each(lambda p, r: jnp.sqrt((p + 2.0 * r) * 0.125) * (4.0 / 64.0), diag, off)
        uh = [each(lambda p: p * (1.0 / 64.0), hat(v_ref, c, x + 1)) for c in range(3)]
        lm = mm = None
        for c in range(6):
            ms = hat(s_ref, 6 + c, x)
            m = each(lambda p, r, g: (p - g * r) * (1.0 / 128.0), ms, s[c], smag4)
            uu = hat(s_ref, 12 + c, x)
            ll = each(
                lambda p, r, g: p * (1.0 / 64.0) - r * g, uu, uh[PAIRS[c][0]], uh[PAIRS[c][1]]
            )
            m2 = m if c < 3 else add(m, m)
            dl, dm = mul(ll, m2), mul(m, m2)
            lm = dl if lm is None else add(lm, dl)
            mm = dm if mm is None else add(mm, dm)

        speed = [each(lambda p: DT * p, get(v_ref, c, x + 2)) for c in range(3)]
        moved = []
        for f in range(2):
            g = get(h_ref, f, x + 1)
            lower, upper = get(h_ref, f, x), get(h_ref, f, x + 2)

            def carry(mid, low, up, sp):
                return each(
                    lambda p, lo, hi, v: p + jnp.abs(v) * (jnp.where(v > 0, lo, hi) - p),
                    mid, low, up, sp,
                )

            g = carry(g, lower, upper, speed[0])
            g = carry(own(g), own(y_prev(g)), own(y_next(g)), own(speed[1]))
            g = carry(g, z_prev(g, first, 0.0), z_next(g, last, 0.0), own(speed[2]))
            moved.append(g)
        k = DT / 1.5
        for z, cols in enumerate(halves):
            m0, m1 = moved[0][z], moved[1][z]
            r = lax.rsqrt(lax.rsqrt(lax.rsqrt(m0 * m1)))
            blend = k / (r + k)
            hit = hit_ref[z, pl.ds(pl.multiple_of(x * NYL, NYL), NYL), :] > 0.5
            new_lm = jnp.maximum(m0 + blend * (lm[z] - m0), 0.0)
            new_mm = m1 + blend * (mm[z] - m1)
            new_ref[0, x, :, cols] = jnp.where(hit, 0.0, new_lm)
            new_ref[1, x, :, cols] = jnp.where(hit, 0.0, new_mm)
        return 0

    lax.fori_loop(0, NXL, close_layer, 0)


def stencil(vel, hist, xl, xr, below, above, dest, weight):
    return pl.pallas_call(
        stencil_kernel,
        in_specs=[pl.BlockSpec(memory_space=pl.ANY)] * 4 + in_vmem(2) + [pl.BlockSpec(memory_space=pl.ANY)] * 2,
        out_specs=in_vmem(3),
        out_shape=[
            jax.ShapeDtypeStruct((2, NXL, NYL, NZ), F32),
            jax.ShapeDtypeStruct((NXL, NYL, NZ), F32),
            jax.ShapeDtypeStruct((8 + PEERS, ROW), F32),
        ],
        scratch_shapes=[
            pltpu.VMEM((3, 12, 2, EXT, ROW), F32),
            pltpu.VMEM((2, 10, 2, EXT, ROW), F32),
            pltpu.VMEM((18, 10, 2, EXT, ROW), F32),
            pltpu.VMEM((2, 32, NZ), F32),
            pltpu.VMEM((2, ROWS // 2, ROW), F32),
            pltpu.VMEM((CAP, PEERS), jnp.int32),
            pltpu.VMEM((CAP, PEERS), F32),
            pltpu.SemaphoreType.DMA((40,)),
        ],
        compiler_params=params(16),
        name="stencil",
        cost_estimate=pl.CostEstimate(
            flops=STENCIL_COST, transcendentals=500_000, bytes_accessed=20_000_000
        ),
    )(vel, hist, xl, xr, below, above, dest, weight)


def place_kernel(new_ref, mag_ref, table_ref, got_ref, out_hbm, eddy_hbm, out_ref, eddy_ref, sems):
    n = 2 * NYL
    place = jnp.concatenate([table_ref[0:1, :], table_ref[1:2, :]], axis=1)
    rows = lax.broadcasted_iota(jnp.int32, (2 * n, CAP * PEERS), 0)
    rows = (rows + jnp.where(rows >= n, ROWS // 2 - n, 0)).astype(F32)
    blended = []
    for c in range(CAP):
        wc = table_ref[8:, c : c + 1]
        cols = []
        for f in range(2):
            r0, r1 = got_ref[:, f * 4 + c * 2, :], got_ref[:, f * 4 + c * 2 + 1, :]
            cols.append(wc * r0 + (1.0 - wc) * r1)
        blended.append(jnp.concatenate(cols, axis=1))
    parts = jnp.concatenate(split3(jnp.concatenate(blended, axis=0)), axis=0)
    copies = []
    for stage in range(NXL // 2):
        onehot = jnp.where(rows + float(stage * n) == place, 1.0, 0.0).astype(BF16)
        acc = jnp.dot(
            jnp.concatenate([onehot] * 3, axis=1), parts, preferred_element_type=F32
        )
        layers = slice(stage * 2, stage * 2 + 2)
        at = pl.ds(stage * 2, 2)
        final = {}
        for h in range(2):
            cols = slice(h * ROW, (h + 1) * ROW)
            for f in range(2):
                cur = new_ref[f, layers, :, cols].reshape(n, ROW)
                val = cur + acc[h * n : (h + 1) * n, f * ROW : (f + 1) * ROW]
                out_ref[f, layers, :, cols] = val.reshape(2, NYL, ROW)
                final[f, h] = val
        copies.append(
            pltpu.make_async_copy(out_ref.at[:, at], out_hbm.at[:, at], sems.at[0, stage])
        )
        copies[-1].start()
        for h in range(2):
            cols = slice(h * ROW, (h + 1) * ROW)
            eddy = final[0, h] / final[1, h] * mag_ref[layers, :, cols].reshape(n, ROW)
            eddy_ref[layers, :, cols] = eddy.reshape(2, NYL, ROW)
        copies.append(pltpu.make_async_copy(eddy_ref.at[at], eddy_hbm.at[at], sems.at[1, stage]))
        copies[-1].start()
    for copy in copies:
        copy.wait()


def place_rows(new, mag, table, got):
    return pl.pallas_call(
        place_kernel,
        in_specs=in_vmem(4),
        out_specs=[pl.BlockSpec(memory_space=pl.ANY)] * 2,
        out_shape=[
            jax.ShapeDtypeStruct((2, NXL, NYL, NZ), F32),
            jax.ShapeDtypeStruct((NXL, NYL, NZ), F32),
        ],
        scratch_shapes=[
            pltpu.VMEM((2, NXL, NYL, NZ), F32),
            pltpu.VMEM((NXL, NYL, NZ), F32),
            pltpu.SemaphoreType.DMA((2, 4)),
        ],
        compiler_params=params(12),
        name="place_receptors",
        cost_estimate=pl.CostEstimate(
            flops=300_000_000, transcendentals=100_000, bytes_accessed=2_500_000
        ),
    )(new, mag, table, got)


def body(velocity, history, donor_rows, recv_dest, recv_weight):
    vel, hist = velocity[:, 0], history[:, 0]
    idx = jnp.transpose(donor_rows[0, 0, 0], (1, 2, 0)).reshape(2 * CAP, PEERS)

    up, down = edges(vel, hist)
    below = shift_ring(up, "span", 1)
    above = shift_ring(down, "span", -1)

    chosen = gather(hist, idx)
    chosen = lax.ppermute(chosen, "grid", [(0, 1), (1, 0)])
    chosen = chosen.reshape(PEERS, 1, 8 * ROW)
    got = lax.all_to_all(chosen, ("stream", "span"), split_axis=0, concat_axis=0, tiled=True)
    got = got.reshape(PEERS, 8, ROW)

    right, left = faces(vel, hist, below, above)
    xl = shift_ring(right, "stream", 1)
    xr = shift_ring(left, "stream", -1)
    dest = jnp.transpose(recv_dest[0, 0, 0])
    weight = jnp.transpose(recv_weight[0, 0, 0])
    made = stencil(vel, hist, xl, xr, below, above, dest, weight)
    final, eddy = place_rows(*made, got)
    return final[:, None], eddy[None]


def solution(mesh):
    in_specs = (
        P(None, "grid", "stream", "span", None),
        P(None, "grid", "stream", "span", None),
        P("grid", "stream", "span", None, None, None),
        P("grid", "stream", "span", None, None),
        P("grid", "stream", "span", None, None),
    )
    out_specs = (P(None, "grid", "stream", "span", None), P("grid", "stream", "span", None))
    return jax.shard_map(body, mesh=mesh, in_specs=in_specs, out_specs=out_specs, check_vma=False)
```

```python
import jax
import jax.numpy as jnp
from jax import lax
from jax.experimental import pallas as pl
from jax.experimental.pallas import tpu as pltpu
from jax.sharding import PartitionSpec as P

F32 = jnp.float32
BF16 = jnp.bfloat16
NXL, NYL, NZ, ROW = 8, 32, 256, 128
ROWS = 512
PEERS = 128
CAP = 2
FACE = 8 * NYL
EDGE_ROOM = 10500 * 1024
FACE_COST = 10_000_000_000
STENCIL_COST = 10_000_000_000
EXT = 40
DT = 0.2
MIB = 1024 * 1024
PAIRS = ((0, 0), (1, 1), (2, 2), (0, 1), (0, 2), (1, 2))


def in_vmem(n):
    return [pl.BlockSpec(memory_space=pltpu.VMEM)] * n


def params(mib):
    return pltpu.CompilerParams(vmem_limit_bytes=mib * MIB)


def shift_ring(x, axis, step):
    n = lax.axis_size(axis)
    return lax.ppermute(x, axis, [(i, (i + step) % n) for i in range(n)])


def split3(x):
    hi = x.astype(BF16)
    rest = x - hi.astype(F32)
    mid = rest.astype(BF16)
    low = (rest - mid.astype(F32)).astype(BF16)
    return hi, mid, low


def gather_kernel(hist_ref, idx_hbm, out_ref, idx_ref, sem):
    copy = pltpu.make_async_copy(idx_hbm, idx_ref, sem)
    copy.start()
    halves = []
    for h in range(2):
        cols = [
            hist_ref[f, :, :, h * ROW : (h + 1) * ROW].reshape(NXL * NYL, ROW)
            for f in range(2)
        ]
        halves.extend(split3(jnp.concatenate(cols, axis=1)))
    table = jnp.concatenate(halves, axis=0)
    copy.wait()
    idx = idx_ref[...]
    place = (idx % 2) * (ROWS // 2) + idx // 2
    place = jnp.transpose(jnp.concatenate([place, place], axis=0).astype(F32))
    lanes = lax.broadcasted_iota(jnp.int32, (PEERS, ROWS // 2), 1).astype(F32)
    for j in range(2 * CAP):
        col = place[:, j : j + 1]
        onehots = []
        for h in range(2):
            onehot = jnp.where(lanes + float(h * ROWS // 2) == col, 1.0, 0.0).astype(BF16)
            onehots += [onehot] * 3
        acc = jnp.dot(jnp.concatenate(onehots, axis=1), table, preferred_element_type=F32)
        for f in range(2):
            out_ref[:, f * 4 + j, :] = acc[:, f * ROW : (f + 1) * ROW]


def gather(hist, idx):
    return pl.pallas_call(
        gather_kernel,
        in_specs=in_vmem(1) + [pl.BlockSpec(memory_space=pl.ANY)],
        out_specs=in_vmem(1)[0],
        scratch_shapes=[
            pltpu.VMEM((2 * CAP, PEERS), jnp.int32),
            pltpu.SemaphoreType.DMA(()),
        ],
        out_shape=jax.ShapeDtypeStruct((PEERS, 8, ROW), F32),
        compiler_params=params(8),
        name="pick_donors",
        cost_estimate=pl.CostEstimate(
            flops=400_000_000, transcendentals=0, bytes_accessed=1_100_000
        ),
    )(hist, idx)


def edge_kernel(vel_hbm, his_hbm, up_ref, down_ref, sems):
    copies = []
    for side, (out, v_row, h_row) in enumerate(
        ((up_ref, NYL - 2, NYL - 1), (down_ref, 0, 0))
    ):
        for c in range(3):
            copies.append(
                pltpu.make_async_copy(
                    vel_hbm.at[c, :, pl.ds(v_row, 2), :],
                    out.at[:, pl.ds(2 * c, 2), :],
                    sems.at[side, c],
                )
            )
        for f in range(2):
            copies.append(
                pltpu.make_async_copy(
                    his_hbm.at[f, :, pl.ds(h_row, 1), :],
                    out.at[:, pl.ds(6 + f, 1), :],
                    sems.at[side, 3 + f],
                )
            )
    for copy in copies:
        copy.start()
    for copy in copies:
        copy.wait()


def edges(vel, hist):
    shape = jax.ShapeDtypeStruct((NXL, 8, NZ), F32)
    return pl.pallas_call(
        edge_kernel,
        in_specs=[pl.BlockSpec(memory_space=pl.ANY)] * 2,
        out_specs=in_vmem(2),
        out_shape=[shape, shape],
        scratch_shapes=[
            pltpu.SemaphoreType.DMA((2, 5)),
        ],
        compiler_params=pltpu.CompilerParams(vmem_limit_bytes=64 * MIB - EDGE_ROOM),
        name="edge_rows",
        cost_estimate=pl.CostEstimate(flops=100_000, transcendentals=0, bytes_accessed=1_000_000),
    )(vel, hist)


def span_keeps():
    b = lax.axis_index("span")
    keep_above = jnp.where(b == lax.axis_size("span") - 1, 0.0, 1.0)
    return jnp.where(b == 0, 0.0, 1.0), keep_above


def face_kernel(vel_ref, his_ref, below_ref, above_ref, right_ref, left_ref):
    a = lax.axis_index("stream")
    last = lax.axis_size("stream") - 1
    keep_below, keep_above = span_keeps()
    for out_ref, first, hist_layer, keep in (
        (right_ref, NXL - 2, NXL - 1, jnp.where(a == last, 0.0, 1.0)),
        (left_ref, 0, 0, jnp.where(a == 0, 0.0, 1.0)),
    ):
        for k in range(8):
            if k < 6:
                c, layer = k // 2, first + k % 2
                plane = vel_ref[c, layer]
                rows = slice(c * 2, c * 2 + 2)
                up, down = above_ref[layer, rows, :], below_ref[layer, rows, :]
            else:
                layer = hist_layer
                plane = his_ref[k - 6, layer]
                up, down = above_ref[layer, k : k + 1, :], below_ref[layer, k : k + 1, :]
            out_ref[k * NYL : (k + 1) * NYL, :] = plane * keep
            base, n = FACE + 4 * k, up.shape[0]
            out_ref[base : base + n, :] = up * (keep * keep_above)
            out_ref[base + 4 - n : base + 4, :] = down * (keep * keep_below)
            if n == 1:
                out_ref[base + 1 : base + 3, :] = jnp.zeros((2, NZ), F32)


def faces(vel, hist, below, above):
    shape = jax.ShapeDtypeStruct((FACE + 32, NZ), F32)
    return pl.pallas_call(
        face_kernel,
        in_specs=in_vmem(4),
        out_specs=in_vmem(2),
        out_shape=[shape, shape],
        compiler_params=params(4),
        name="face_layers",
        cost_estimate=pl.CostEstimate(flops=FACE_COST, transcendentals=0, bytes_accessed=1_200_000),
    )(vel, hist, below, above)


def add(a, b):
    return tuple(p + q for p, q in zip(a, b))


def sub(a, b):
    return tuple(p - q for p, q in zip(a, b))


def mul(a, b):
    return tuple(p * q for p, q in zip(a, b))


def each(fn, *a):
    return tuple(fn(*p) for p in zip(*a))


def y_next(a):
    return tuple(pltpu.roll(p, EXT - 1, 0) for p in a)


def y_prev(a):
    return tuple(pltpu.roll(p, 1, 0) for p in a)


def own(a):
    return tuple(p[:NYL] for p in a)


def z_prev(a, first, fill):
    lo, hi = a
    rlo, rhi = pltpu.roll(lo, 1, 1), pltpu.roll(hi, 1, 1)
    m = first[: lo.shape[0]]
    return jnp.where(m, fill, rlo), jnp.where(m, rlo, rhi)


def z_next(a, last, fill):
    lo, hi = a
    rlo, rhi = pltpu.roll(lo, ROW - 1, 1), pltpu.roll(hi, ROW - 1, 1)
    m = last[: lo.shape[0]]
    return jnp.where(m, rhi, rlo), jnp.where(m, fill, rhi)


def placement(dest_ref, w_ref, table_ref, hit_ref):
    dest = dest_ref[...]
    place = jnp.where(dest >= ROWS, -1, (dest % 2) * (ROWS // 2) + dest // 2).astype(F32)
    for c in range(CAP):
        table_ref[c : c + 1, :] = place[c : c + 1]
    table_ref[8:, :] = jnp.zeros((PEERS, ROW), F32)
    table_ref[8:, 0:8] = jnp.transpose(jnp.concatenate([w_ref[...]] * 4, axis=0))
    ones = jnp.ones((CAP * PEERS, ROW), BF16)
    place = jnp.concatenate([place[0:1], place[1:2]], axis=1)
    rows = lax.broadcasted_iota(jnp.int32, (ROWS // 2, CAP * PEERS), 0).astype(F32)
    for h in range(2):
        onehot = jnp.where(rows + float(h * ROWS // 2) == place, 1.0, 0.0).astype(BF16)
        hit_ref[h] = jnp.dot(onehot, ones, preferred_element_type=F32)


def stencil_kernel(
    vel_hbm, his_hbm, xl_hbm, xr_hbm, below_ref, above_ref, dest_hbm, w_hbm,
    new_ref, mag_ref, table_ref,
    v_ref, h_ref, s_ref, corner_ref, hit_ref, dest_ref, w_ref, sems,
):
    a_id = lax.axis_index("stream")
    b_id = lax.axis_index("span")
    a_last = lax.axis_size("stream") - 1
    b_last = lax.axis_size("span") - 1
    halves = (slice(0, ROW), slice(ROW, NZ))

    copies = [
        pltpu.make_async_copy(
            ref.at[pl.ds(FACE, 32), :], corner_ref.at[side], sems.at[side]
        )
        for side, ref in enumerate((xl_hbm, xr_hbm))
    ]
    copies.append(pltpu.make_async_copy(dest_hbm, dest_ref, sems.at[38]))
    copies.append(pltpu.make_async_copy(w_hbm, w_ref, sems.at[39]))
    for z, cols in enumerate(halves):
        lanes = pl.ds(z * ROW, ROW)
        copies.append(
            pltpu.make_async_copy(
                vel_hbm.at[:, :, :, lanes],
                v_ref.at[:, pl.ds(2, NXL), z, pl.ds(0, NYL), :],
                sems.at[2 + z],
            )
        )
        copies.append(
            pltpu.make_async_copy(
                his_hbm.at[:, :, :, lanes],
                h_ref.at[:, pl.ds(1, NXL), z, pl.ds(0, NYL), :],
                sems.at[4 + z],
            )
        )
        for side, ref in enumerate((xl_hbm, xr_hbm)):
            for k in range(8):
                rows = pl.ds(k * NYL, NYL)
                if k < 6:
                    to = v_ref.at[k // 2, side * 10 + k % 2, z, pl.ds(0, NYL), :]
                else:
                    to = h_ref.at[k - 6, side * 9, z, pl.ds(0, NYL), :]
                copies.append(
                    pltpu.make_async_copy(
                        ref.at[rows, lanes], to, sems.at[6 + (side * 2 + z) * 8 + k]
                    )
                )
    for copy in copies:
        copy.start()

    zero4 = jnp.zeros((4, ROW), F32)
    keep_below, keep_above = span_keeps()

    def fill(ref, c, layer, z, up, down):
        n = up.shape[0]
        ref[c, layer, z, NYL : NYL + n, :] = up
        ref[c, layer, z, NYL + n : NYL + n + 4, :] = zero4
        ref[c, layer, z, NYL + 4 : EXT - n, :] = zero4[: 4 - n]
        ref[c, layer, z, EXT - n :, :] = down

    for z, cols in enumerate(halves):
        for layer in range(NXL):
            for c in range(3):
                rows = slice(c * 2, c * 2 + 2)
                up = above_ref[layer, rows, cols] * keep_above
                down = below_ref[layer, rows, cols] * keep_below
                fill(v_ref, c, layer + 2, z, up, down)
            for f in range(2):
                rows = slice(6 + f, 7 + f)
                up = above_ref[layer, rows, cols] * keep_above
                down = below_ref[layer, rows, cols] * keep_below
                fill(h_ref, f, layer + 1, z, up, down)
    for copy in copies:
        copy.wait()
    placement(dest_ref, w_ref, table_ref, hit_ref)
    for z, cols in enumerate(halves):
        for side in range(2):
            for k in range(8):
                n = 2 if k < 6 else 1
                up = corner_ref[side, 4 * k : 4 * k + n, cols]
                down = corner_ref[side, 4 * k + 4 - n : 4 * k + 4, cols]
                if k < 6:
                    fill(v_ref, k // 2, side * 10 + k % 2, z, up, down)
                else:
                    fill(h_ref, k - 6, side * 9, z, up, down)

    lane = lax.broadcasted_iota(jnp.int32, (EXT, ROW), 1)
    first, last = lane == 0, lane == ROW - 1
    row = lax.broadcasted_iota(jnp.int32, (EXT, ROW), 0)
    inside = jnp.where((row == 32) & (b_id == b_last), 0.0, 1.0) * jnp.where(
        (row == 39) & (b_id == 0), 0.0, 1.0
    )

    def get(ref, c, layer):
        return ref[c, layer, 0], ref[c, layer, 1]

    def smooth(below, mid, above):
        t = add(add(below, mid), add(mid, above))
        t = add(t, y_next(t))
        t = own(add(t, y_prev(t)))
        return add(add(t, t), add(z_prev(t, first, 0.0), z_next(t, last, 0.0)))

    def strain_layer(i, _):
        u = [get(v_ref, c, i + 1) for c in range(3)]
        keep = jnp.where(((i == 0) & (a_id == 0)) | ((i == 9) & (a_id == a_last)), 0.0, 1.0)
        m = inside * keep
        gx = [sub(get(v_ref, c, i + 2), get(v_ref, c, i)) for c in range(3)]
        gy = [sub(y_next(p), y_prev(p)) for p in u]
        gz = [sub(z_next(p, last, 0.0), z_prev(p, first, 0.0)) for p in u]
        t = [
            add(gx[0], gx[0]),
            add(gy[1], gy[1]),
            add(gz[2], gz[2]),
            add(gy[0], gx[1]),
            add(gz[0], gx[2]),
            add(gz[1], gy[2]),
        ]
        t = [each(lambda p: p * m, p) for p in t]
        q = [mul(p, p) for p in t]
        diag = add(add(q[0], q[1]), q[2])
        off = add(add(q[3], q[4]), q[5])
        mag = each(lambda p, r: jnp.sqrt((p + 2.0 * r) * 0.125), diag, off)

        @pl.when((i >= 1) & (i <= 8))
        def _():
            for z, cols in enumerate(halves):
                mag_ref[i - 1, :, cols] = mag[z][:NYL]

        for c in range(6):
            w = mul(mag, t[c])
            uu = mul(u[PAIRS[c][0]], u[PAIRS[c][1]])
            for z in range(2):
                s_ref[c, i, z] = t[c][z]
                s_ref[6 + c, i, z] = w[z]
                s_ref[12 + c, i, z] = uu[z]
        return 0

    lax.fori_loop(0, 10, strain_layer, 0)

    def close_layer(x, _):
        def hat(ref, c, at):
            return smooth(get(ref, c, at), get(ref, c, at + 1), get(ref, c, at + 2))

        s = [hat(s_ref, c, x) for c in range(6)]
        q = [mul(p, p) for p in s]
        diag = add(add(q[0], q[1]), q[2])
        off = add(add(q[3], q[4]), q[5])
        smag4 = each(lambda p, r: jnp.sqrt((p + 2.0 * r) * 0.125) * (4.0 / 64.0), diag, off)
        uh = [each(lambda p: p * (1.0 / 64.0), hat(v_ref, c, x + 1)) for c in range(3)]
        lm = mm = None
        for c in range(6):
            ms = hat(s_ref, 6 + c, x)
            m = each(lambda p, r, g: (p - g * r) * (1.0 / 128.0), ms, s[c], smag4)
            uu = hat(s_ref, 12 + c, x)
            ll = each(
                lambda p, r, g: p * (1.0 / 64.0) - r * g, uu, uh[PAIRS[c][0]], uh[PAIRS[c][1]]
            )
            m2 = m if c < 3 else add(m, m)
            dl, dm = mul(ll, m2), mul(m, m2)
            lm = dl if lm is None else add(lm, dl)
            mm = dm if mm is None else add(mm, dm)

        speed = [each(lambda p: DT * p, get(v_ref, c, x + 2)) for c in range(3)]
        moved = []
        for f in range(2):
            g = get(h_ref, f, x + 1)
            lower, upper = get(h_ref, f, x), get(h_ref, f, x + 2)

            def carry(mid, low, up, sp):
                return each(
                    lambda p, lo, hi, v: p + jnp.abs(v) * (jnp.where(v > 0, lo, hi) - p),
                    mid, low, up, sp,
                )

            g = carry(g, lower, upper, speed[0])
            g = carry(own(g), own(y_prev(g)), own(y_next(g)), own(speed[1]))
            g = carry(g, z_prev(g, first, 0.0), z_next(g, last, 0.0), own(speed[2]))
            moved.append(g)
        k = DT / 1.5
        for z, cols in enumerate(halves):
            m0, m1 = moved[0][z], moved[1][z]
            r = lax.rsqrt(lax.rsqrt(lax.rsqrt(m0 * m1)))
            blend = k / (r + k)
            hit = hit_ref[z, pl.ds(pl.multiple_of(x * NYL, NYL), NYL), :] > 0.5
            new_lm = jnp.maximum(m0 + blend * (lm[z] - m0), 0.0)
            new_mm = m1 + blend * (mm[z] - m1)
            new_ref[0, x, :, cols] = jnp.where(hit, 0.0, new_lm)
            new_ref[1, x, :, cols] = jnp.where(hit, 0.0, new_mm)
        return 0

    lax.fori_loop(0, NXL, close_layer, 0)


def stencil(vel, hist, xl, xr, below, above, dest, weight):
    return pl.pallas_call(
        stencil_kernel,
        in_specs=[pl.BlockSpec(memory_space=pl.ANY)] * 4 + in_vmem(2) + [pl.BlockSpec(memory_space=pl.ANY)] * 2,
        out_specs=in_vmem(3),
        out_shape=[
            jax.ShapeDtypeStruct((2, NXL, NYL, NZ), F32),
            jax.ShapeDtypeStruct((NXL, NYL, NZ), F32),
            jax.ShapeDtypeStruct((8 + PEERS, ROW), F32),
        ],
        scratch_shapes=[
            pltpu.VMEM((3, 12, 2, EXT, ROW), F32),
            pltpu.VMEM((2, 10, 2, EXT, ROW), F32),
            pltpu.VMEM((18, 10, 2, EXT, ROW), F32),
            pltpu.VMEM((2, 32, NZ), F32),
            pltpu.VMEM((2, ROWS // 2, ROW), F32),
            pltpu.VMEM((CAP, PEERS), jnp.int32),
            pltpu.VMEM((CAP, PEERS), F32),
            pltpu.SemaphoreType.DMA((40,)),
        ],
        compiler_params=params(16),
        name="stencil",
        cost_estimate=pl.CostEstimate(
            flops=STENCIL_COST, transcendentals=500_000, bytes_accessed=20_000_000
        ),
    )(vel, hist, xl, xr, below, above, dest, weight)


def place_kernel(new_ref, mag_ref, table_ref, got_ref, out_hbm, eddy_hbm, out_ref, eddy_ref, sems):
    n = 2 * NYL
    place = jnp.concatenate([table_ref[0:1, :], table_ref[1:2, :]], axis=1)
    rows = lax.broadcasted_iota(jnp.int32, (2 * n, CAP * PEERS), 0)
    rows = (rows + jnp.where(rows >= n, ROWS // 2 - n, 0)).astype(F32)
    blended = []
    for c in range(CAP):
        wc = table_ref[8:, c : c + 1]
        cols = []
        for f in range(2):
            r0, r1 = got_ref[:, f * 4 + c * 2, :], got_ref[:, f * 4 + c * 2 + 1, :]
            cols.append(r1 + wc * (r0 - r1))
        blended.append(jnp.concatenate(cols, axis=1))
    parts = jnp.concatenate(split3(jnp.concatenate(blended, axis=0)), axis=0)
    copies = []
    for stage in range(NXL // 2):
        onehot = jnp.where(rows + float(stage * n) == place, 1.0, 0.0).astype(BF16)
        acc = jnp.dot(
            jnp.concatenate([onehot] * 3, axis=1), parts, preferred_element_type=F32
        )
        layers = slice(stage * 2, stage * 2 + 2)
        at = pl.ds(stage * 2, 2)
        for h in range(2):
            cols = slice(h * ROW, (h + 1) * ROW)
            final = []
            for f in range(2):
                cur = new_ref[f, layers, :, cols].reshape(n, ROW)
                val = cur + acc[h * n : (h + 1) * n, f * ROW : (f + 1) * ROW]
                out_ref[f, layers, :, cols] = val.reshape(2, NYL, ROW)
                final.append(val)
            eddy = final[0] / final[1] * mag_ref[layers, :, cols].reshape(n, ROW)
            eddy_ref[layers, :, cols] = eddy.reshape(2, NYL, ROW)
        copies.append(
            pltpu.make_async_copy(out_ref.at[:, at], out_hbm.at[:, at], sems.at[0, stage])
        )
        copies.append(pltpu.make_async_copy(eddy_ref.at[at], eddy_hbm.at[at], sems.at[1, stage]))
        copies[-2].start()
        copies[-1].start()
    for copy in copies:
        copy.wait()


def place_rows(new, mag, table, got):
    return pl.pallas_call(
        place_kernel,
        in_specs=in_vmem(4),
        out_specs=[pl.BlockSpec(memory_space=pl.ANY)] * 2,
        out_shape=[
            jax.ShapeDtypeStruct((2, NXL, NYL, NZ), F32),
            jax.ShapeDtypeStruct((NXL, NYL, NZ), F32),
        ],
        scratch_shapes=[
            pltpu.VMEM((2, NXL, NYL, NZ), F32),
            pltpu.VMEM((NXL, NYL, NZ), F32),
            pltpu.SemaphoreType.DMA((2, 4)),
        ],
        compiler_params=params(12),
        name="place_receptors",
        cost_estimate=pl.CostEstimate(
            flops=300_000_000, transcendentals=100_000, bytes_accessed=2_500_000
        ),
    )(new, mag, table, got)


def body(velocity, history, donor_rows, recv_dest, recv_weight):
    vel, hist = velocity[:, 0], history[:, 0]
    idx = jnp.transpose(donor_rows[0, 0, 0], (1, 2, 0)).reshape(2 * CAP, PEERS)

    up, down = edges(vel, hist)
    below = shift_ring(up, "span", 1)
    above = shift_ring(down, "span", -1)

    chosen = gather(hist, idx)
    chosen = lax.ppermute(chosen, "grid", [(0, 1), (1, 0)])
    chosen = chosen.reshape(PEERS, 1, 8 * ROW)
    got = lax.all_to_all(chosen, ("stream", "span"), split_axis=0, concat_axis=0, tiled=True)
    got = got.reshape(PEERS, 8, ROW)

    right, left = faces(vel, hist, below, above)
    xl = shift_ring(right, "stream", 1)
    xr = shift_ring(left, "stream", -1)
    dest = jnp.transpose(recv_dest[0, 0, 0])
    weight = jnp.transpose(recv_weight[0, 0, 0])
    made = stencil(vel, hist, xl, xr, below, above, dest, weight)
    final, eddy = place_rows(*made, got)
    return final[:, None], eddy[None]


def solution(mesh):
    in_specs = (
        P(None, "grid", "stream", "span", None),
        P(None, "grid", "stream", "span", None),
        P("grid", "stream", "span", None, None, None),
        P("grid", "stream", "span", None, None),
        P("grid", "stream", "span", None, None),
    )
    out_specs = (P(None, "grid", "stream", "span", None), P("grid", "stream", "span", None))
    return jax.shard_map(body, mesh=mesh, in_specs=in_specs, out_specs=out_specs, check_vma=False)
```
